128 devices in a mesh: dp: 8 (over z, core), et: 16 (over y, x).
Axes of the slice: x: 4, y: 4, z: 4, core: 2. Of those that a mesh axis runs over, the one named last changes fastest.
Arguments:
- routed_rows: bfloat16 [4096, 4096], P(('dp', 'et')), may hold values from -6 to 6
- out_cotangent: bfloat16 [4096, 4096], P(('dp', 'et')), may hold values from -6 to 6
- route_weight: float32 [4096], P(('dp', 'et')), may hold values from 0.1 to 1
- expert_counts: int32 [8, 2], replicated, may hold values from 1 to 256, as said below
- w_gate: bfloat16 [2, 4096, 7168], P(None, None, 'et'), may hold values from -0.09375 to 0.09375
- w_up: bfloat16 [2, 4096, 7168], P(None, None, 'et'), may hold values from -0.09375 to 0.09375
- w_down: bfloat16 [2, 7168, 4096], P(None, 'et'), may hold values from -0.0625 to 0.0625
Outputs:
- layer_out: bfloat16 [4096, 4096], P(('dp', 'et'))
- grad_weight: float32 [4096], P(('dp', 'et'))
- grad_rows: bfloat16 [4096, 4096], P(('dp', 'et'))
- grad_gate: bfloat16 [2, 4096, 7168], P(None, 'dp', 'et')
- grad_up: bfloat16 [2, 4096, 7168], P(None, 'dp', 'et')
- grad_down: bfloat16 [2, 7168, 4096], P(None, 'et', 'dp')
The draws below stay inside these ranges and needn't reach their ends.
Inputs may be any that keep to these rules, and one draw needn't show every extreme that they name: `expert_counts`: both counts of a group, each rounded up to a multiple of 128, sum to at most 512; in some group both counts equal 256.
All inputs are finite; a program needn't handle non-finite values.
Results may differ from the reference program's by a relative error of at most 0.029.
Values may be sent and summed in bfloat16 or wider, within the bound.
A program may use at most 192 MiB of HBM per device.

```python
import jax
import jax.numpy as jnp
from jax import lax

D = 4096
FFW = 7168
EXP = 2
BLOCK = 128
SLOTS = 512
GROUPS = 8
ROWS = 4096
N_ET = 16


def draw_expert_counts(key, part):
    key_busy, key_total, key_split = jax.random.split(jax.random.fold_in(key, 17), 3)
    busiest = jax.random.randint(key_busy, (), 0, GROUPS)
    totals = jax.random.randint(key_total, (GROUPS,), SLOTS // 16, 3 * SLOTS // 8)
    first_count = jax.random.randint(key_split, (GROUPS,), 1, totals)
    second_count = totals - first_count
    ranks = jnp.arange(GROUPS, dtype=jnp.int32)
    first_count = jnp.where(ranks == busiest, SLOTS // 2, first_count)
    second_count = jnp.where(ranks == busiest, SLOTS // 2, second_count)
    return jnp.stack([first_count, second_count], axis=1).astype(jnp.int32)


def block_levels(rng, dims, cuts, least, largest):
    factor_of = 1.0
    for dim, shards_of in cuts:
        heights = jax.random.uniform(jax.random.fold_in(jax.random.fold_in(rng, 6), dim), (shards_of,), jnp.float32, least / len(cuts), largest / len(cuts))
        factor_of = factor_of * jnp.repeat(jnp.exp(heights), dims[dim] // shards_of).reshape((-1,) + (1,) * (len(dims) - 1 - dim))
    return factor_of


def noise(own_key, shape, scale, bound, cuts=(), kind=jnp.bfloat16):
    gain = block_levels(own_key, shape, cuts, -0.22, 0.18) if cuts else 1.0
    drawn = jax.random.normal(own_key, shape, jnp.float32) * scale * gain
    return jnp.minimum(jnp.maximum(drawn, -bound), bound).astype(kind)


def setup_inputs(seed: int = 0) -> dict:
    arg_keys = jax.random.split(jax.random.key(seed), 8)
    routed_rows = noise(arg_keys[0], (ROWS, D), 1.0, 6.0, ((0, 128),))
    out_cotangent = noise(arg_keys[1], (ROWS, D), 1.0, 6.0, ((0, 128),))
    route_weight = jnp.clip(0.1 + 0.9 * jax.random.uniform(arg_keys[2], (ROWS,), jnp.float32) ** block_levels(arg_keys[2], (ROWS,), ((0, 128),), -0.2, 0.2), 0.1, 1.0)
    expert_counts = draw_expert_counts(jax.random.fold_in(arg_keys[7], 71), 0)
    w_gate = noise(arg_keys[4], (EXP, D, FFW), D ** -0.5, 0.09375, ((2, 16),))
    w_up = noise(arg_keys[5], (EXP, D, FFW), D ** -0.5, 0.09375, ((2, 16),))
    w_down = noise(arg_keys[6], (EXP, FFW, D), FFW ** -0.5, 0.0625, ((1, 16),))
    return dict(routed_rows=routed_rows, out_cotangent=out_cotangent, route_weight=route_weight, expert_counts=expert_counts, w_gate=w_gate, w_up=w_up, w_down=w_down)


def block_layout(counts_row):
    padded = ((counts_row + BLOCK - 1) // BLOCK * BLOCK).astype(jnp.int32)
    starts = (jnp.cumsum(padded) - padded).astype(jnp.int32)
    position = jnp.arange(SLOTS, dtype=jnp.int32)
    relative = position[:, None] - starts[None, :]
    live_rows = jnp.any((relative >= 0) & (relative < counts_row[None, :]), axis=1)
    block_first = jnp.arange(SLOTS // BLOCK, dtype=jnp.int32) * BLOCK
    block_rel = block_first[:, None] - starts[None, :]
    owned = (block_rel >= 0) & (block_rel < padded[None, :])
    expert_ids = jnp.arange(counts_row.shape[0], dtype=jnp.int32)
    block_expert = jnp.sum(jnp.where(owned, expert_ids[None, :], 0), axis=1).astype(jnp.int32)
    return live_rows, block_expert


def rounded_parts(left, right_t, share_width):
    model_width = right_t.shape[1]
    terms = jnp.einsum("bsf,sfd->bsd", left.astype(jnp.float32).reshape(left.shape[0], N_ET, share_width),
                       right_t.astype(jnp.float32).reshape(N_ET, share_width, model_width))
    return terms


def reference(routed_rows, out_cotangent, route_weight, expert_counts, w_gate, w_up, w_down):
    model_width = routed_rows.shape[1]
    hidden_width = w_gate.shape[2]
    share_width = hidden_width // N_ET
    block_count = SLOTS // BLOCK
    out_list, weight_list, rows_list = [], [], []
    total_gate = jnp.zeros(w_gate.shape, jnp.float32)
    total_lin = jnp.zeros(w_up.shape, jnp.float32)
    total_down = jnp.zeros(w_down.shape, jnp.float32)
    for group_index in range(GROUPS):
        row_first = group_index * SLOTS
        rows_here = routed_rows[row_first:row_first + SLOTS]
        cot_here = out_cotangent[row_first:row_first + SLOTS]
        weight_here = route_weight[row_first:row_first + SLOTS]
        live_rows, block_expert = block_layout(expert_counts[group_index])
        row_blocks = rows_here.reshape(block_count, BLOCK, model_width)
        mask_blocks = live_rows.reshape(block_count, BLOCK, 1)

        def forward_block(operands):
            row_block, mask_block, expert = operands
            gate_pre = jnp.dot(row_block, w_gate[expert], preferred_element_type=jnp.float32)
            lin_pre = jnp.dot(row_block, w_up[expert], preferred_element_type=jnp.float32)
            hidden = jnp.where(mask_block, jax.nn.silu(gate_pre) * lin_pre, 0.0).astype(jnp.bfloat16)
            terms = rounded_parts(hidden, w_down[expert], share_width)
            terms = lax.optimization_barrier(terms.astype(jnp.bfloat16)).astype(jnp.float32)
            return gate_pre, lin_pre, hidden, jnp.sum(terms, axis=1)

        gate_pre, lin_pre, hidden, combined = lax.map(forward_block, (row_blocks, mask_blocks, block_expert))
        combined = combined.reshape(SLOTS, model_width)
        out_list.append((weight_here[:, None] * combined).astype(jnp.bfloat16))
        weight_list.append(jnp.sum(cot_here.astype(jnp.float32) * combined, axis=1))
        scaled = (weight_here[:, None] * cot_here.astype(jnp.float32)).astype(jnp.bfloat16)
        scaled_blocks = scaled.reshape(block_count, BLOCK, model_width)

        def backward_block(operands):
            scaled_block, gate_block, lin_block, mask_block, expert = operands
            grad_hidden = jnp.dot(scaled_block, jnp.transpose(w_down[expert]), preferred_element_type=jnp.float32)
            logistic = jax.nn.sigmoid(gate_block)
            grad_gate_pre = jnp.where(mask_block, grad_hidden * lin_block * logistic * (1.0 + gate_block * (1.0 - logistic)), 0.0).astype(jnp.bfloat16)
            grad_lin_pre = jnp.where(mask_block, grad_hidden * gate_block * logistic, 0.0).astype(jnp.bfloat16)
            terms = rounded_parts(grad_gate_pre, jnp.transpose(w_gate[expert]), share_width)
            terms = terms + rounded_parts(grad_lin_pre, jnp.transpose(w_up[expert]), share_width)
            terms = lax.optimization_barrier(terms.astype(jnp.bfloat16)).astype(jnp.float32)
            return grad_gate_pre, grad_lin_pre, jnp.sum(terms, axis=1)

        grad_gate_pre, grad_lin_pre, rows_grad = lax.map(backward_block, (scaled_blocks, gate_pre, lin_pre, mask_blocks, block_expert))
        rows_list.append(rows_grad.reshape(SLOTS, model_width).astype(jnp.bfloat16))
        gate_flat = grad_gate_pre.reshape(SLOTS, hidden_width)
        lin_flat = grad_lin_pre.reshape(SLOTS, hidden_width)
        hidden_flat = hidden.reshape(SLOTS, hidden_width)
        row_expert = jnp.repeat(block_expert, BLOCK)
        gate_terms, lin_terms, down_terms = [], [], []
        for expert in range(EXP):
            chosen = (row_expert == expert)[:, None]
            gate_terms.append(jnp.dot(jnp.transpose(rows_here), jnp.where(chosen, gate_flat, jnp.zeros_like(gate_flat)), preferred_element_type=jnp.float32))
            lin_terms.append(jnp.dot(jnp.transpose(rows_here), jnp.where(chosen, lin_flat, jnp.zeros_like(lin_flat)), preferred_element_type=jnp.float32))
            down_terms.append(jnp.dot(jnp.transpose(jnp.where(chosen, hidden_flat, jnp.zeros_like(hidden_flat))), scaled, preferred_element_type=jnp.float32))
        total_gate = total_gate + lax.optimization_barrier(jnp.stack(gate_terms).astype(jnp.bfloat16)).astype(jnp.float32)
        total_lin = total_lin + lax.optimization_barrier(jnp.stack(lin_terms).astype(jnp.bfloat16)).astype(jnp.float32)
        total_down = total_down + lax.optimization_barrier(jnp.stack(down_terms).astype(jnp.bfloat16)).astype(jnp.float32)
    return (jnp.concatenate(out_list, axis=0), jnp.concatenate(weight_list, axis=0),
            jnp.concatenate(rows_list, axis=0), total_gate.astype(jnp.bfloat16),
            total_lin.astype(jnp.bfloat16), total_down.astype(jnp.bfloat16))
```

```python
import functools

import jax
import jax.numpy as jnp
from jax import lax
from jax.experimental import pallas as pl
from jax.experimental.pallas import tpu as pltpu
from jax.sharding import PartitionSpec as P

MESH = pl.DeviceIdType.MESH
BF = jnp.bfloat16
F32 = jnp.float32
GROUPS, SLOTS, OWN, DM, HID = 8, 512, 32, 4096, 448
DS = DM // GROUPS
ROWS = GROUPS * SLOTS
BR = 256
RMAX = ROWS + BR
LEVELS = (1536, 1792, 2048, RMAX)
VLIM = 60 * 1024 * 1024


def rcopy(src, dst, ssem, rsem, dev):
    return pltpu.make_async_remote_copy(
        src_ref=src, dst_ref=dst, send_sem=ssem, recv_sem=rsem,
        device_id=dev, device_id_type=MESH,
    )


def greet(peers):
    bar = pltpu.get_barrier_semaphore()
    for dev in peers:
        pl.semaphore_signal(bar, inc=1, device_id=dev, device_id_type=MESH)
    pl.semaphore_wait(bar, len(peers))


def plane(axis, pos, j):
    y, x = j // 4, j % 4
    return {"et": y * 4 + pos % 4} if axis == "x" else {"et": (pos % 4) * 4 + x}


def gather_kernel(rows_ref, sc_ref, xg, sg, psend, precv, osem, rsend, rrecv):
    d, j = lax.axis_index("dp"), lax.axis_index("et")
    y, x = j // 4, j % 4
    greet([{"dp": (d + k) % 8} for k in range(1, 8)]
          + [plane("x", x + 1, j), plane("x", x + 3, j), plane("y", y + 1, j), plane("y", y + 3, j)])
    arrays = []
    for a, (src, out, first, second) in enumerate(
        ((rows_ref, xg, "x", "y"), (sc_ref, sg, "y", "x"))
    ):
        p, q = (x, y) if first == "x" else (y, x)

        def blk(pp, qq, half=None, out=out, first=first):
            yy, xx = (qq % 4, pp % 4) if first == "x" else (pp % 4, qq % 4)
            g = slice(None) if half is None else pl.ds(4 * half, 4)
            return out.at[g, yy, xx]

        def send(i, ref, axis, pos, a=a):
            c = rcopy(ref, ref, rsend.at[a, i], rrecv.at[a, i], plane(axis, pos, j))
            c.start()
            return c

        cps = []
        for k in range(1, 8):
            dd = (d + k) % 8
            c = rcopy(src.at[:, pl.ds(dd * DS, DS)], out.at[d, y, x],
                      psend.at[a, k - 1], precv.at[a, k - 1], {"dp": dd})
            c.start()
            cps.append(c)
        own = pltpu.make_async_copy(src.at[:, pl.ds(d * DS, DS)], out.at[d, y, x], osem.at[a])
        own.start()
        arrays.append((p, q, first, second, blk, send, cps, own))

    sent = [dict(), dict()]

    def second_sends(a, u):
        p, q, first, second, blk, send, cps, own = arrays[a]
        base = 4 + 4 * (u % 4)
        sent[a][base] = send(base, blk(p + u, q), second, q + 1)
        sent[a][base + 1] = send(base + 1, blk(p + u, q), second, q + 3)

    def second_forward(a, u):
        p, q, first, second, blk, send, cps, own = arrays[a]
        base = 4 + 4 * (u % 4)
        sent[a][base].wait_recv()
        sent[a][base + 2] = send(base + 2, blk(p + u, q + 3, 0), second, q + 1)
        sent[a][base + 1].wait_recv()
        sent[a][base + 3] = send(base + 3, blk(p + u, q + 1, 1), second, q + 3)

    for a in range(2):
        p, q, first, second, blk, send, cps, own = arrays[a]
        own.wait()
        for c in cps:
            c.wait_recv()
        sent[a][0] = send(0, blk(p, q), first, p + 1)
        sent[a][1] = send(1, blk(p, q), first, p + 3)
        second_sends(a, 0)
    for a in range(2):
        p, q, first, second, blk, send, cps, own = arrays[a]
        sent[a][0].wait_recv()
        sent[a][2] = send(2, blk(p + 3, q, 0), first, p + 1)
        second_sends(a, 3)
        sent[a][1].wait_recv()
        sent[a][3] = send(3, blk(p + 1, q, 1), first, p + 3)
        second_sends(a, 1)
    for a in range(2):
        second_forward(a, 0)
    for a in range(2):
        sent[a][2].wait_recv()
        sent[a][3].wait_recv()
        second_sends(a, 2)
    for u in (3, 1, 2):
        for a in range(2):
            second_forward(a, u)
    for a in range(2):
        for u in range(4):
            sent[a][6 + 4 * u].wait_recv()
            sent[a][7 + 4 * u].wait_recv()
        for c in arrays[a][6]:
            c.wait_send()
        for c in sent[a].values():
            c.wait_send()


def gather_rows(rows, scaled):
    shape = jax.ShapeDtypeStruct((GROUPS, 4, 4, OWN, DS), BF)
    return pl.pallas_call(
        gather_kernel,
        out_shape=(shape, shape),
        in_specs=[pl.BlockSpec(memory_space=pltpu.VMEM)] * 2,
        out_specs=(pl.BlockSpec(memory_space=pl.ANY),) * 2,
        scratch_shapes=[
            pltpu.SemaphoreType.DMA((2, 7)),
            pltpu.SemaphoreType.DMA((2, 7)),
            pltpu.SemaphoreType.DMA((2,)),
            pltpu.SemaphoreType.DMA((2, 20)),
            pltpu.SemaphoreType.DMA((2, 20)),
        ],
        compiler_params=pltpu.CompilerParams(
            collective_id=0, has_side_effects=True, vmem_limit_bytes=VLIM),
        name="gather_rows",
    )(rows, scaled)


def segments(cnt):
    segs, t = [], 0
    ends = []
    for e in range(2):
        row = []
        for g in range(GROUPS):
            c = cnt[g, e]
            first = 0 if e == 0 else (cnt[g, 0] + 127) // 128 * 128
            n = (c + 15) // 16
            row.append((c, first, n, t))
            t = t + n
        ends.append(t)
        t = (t + BR // 16 - 1) // (BR // 16) * (BR // 16)
        ends.append(t)
        segs.append(row)
    return segs, ends


def tile(i):
    return pl.ds(pl.multiple_of(i * 16, 16), 16)


def first_kernel(cnt, xg, sg, wg, wu, wd, part, xc_o, sc_o,
                 xv, sv, xc, sc, wgv, wuv, wdv, pv, rsem, wsem, osem):
    d = lax.axis_index("dp")
    cols = pl.ds(pl.multiple_of(d * DS, DS), DS)
    segs, ends = segments(cnt)
    wcp = [pltpu.make_async_copy(wg.at[:, cols, :], wgv, wsem.at[0]),
           pltpu.make_async_copy(wu.at[:, cols, :], wuv, wsem.at[1]),
           pltpu.make_async_copy(wd.at[:, :, cols], wdv, wsem.at[2])]

    def block_copies(g, b):
        rows = pl.ds(g * SLOTS + b * 128, 128)
        return (pltpu.make_async_copy(xg.at[rows], xv.at[rows], rsem.at[0, g * 4 + b]),
                pltpu.make_async_copy(sg.at[rows], sv.at[rows], rsem.at[1, g * 4 + b]))

    for start in (True, False):
        for g in range(GROUPS):
            used = (cnt[g, 0] + 127) // 128 + (cnt[g, 1] + 127) // 128
            for b in range(4):
                @pl.when(b < used)
                def _(g=g, b=b, start=start):
                    for c in block_copies(g, b):
                        if start:
                            c.start()
                        else:
                            c.wait()
        if start:
            for c in wcp:
                c.start()

    zeros = jnp.zeros((16, DS), BF)
    iota = lax.broadcasted_iota(jnp.int32, (16, DS), 0)
    for e in range(2):
        for g in range(GROUPS):
            c, first, n, t0 = segs[e][g]
            s0 = g * (SLOTS // 16) + first // 16

            def move(k, _, s0=s0, t0=t0):
                xc[tile(t0 + k), :] = xv[tile(s0 + k), :]
                sc[tile(t0 + k), :] = sv[tile(s0 + k), :]
                return 0

            lax.fori_loop(0, n - 1, move, 0)
            keep = iota < c - 16 * (n - 1)
            xt = xv[tile(s0 + n - 1), :].astype(F32)
            st = sv[tile(s0 + n - 1), :].astype(F32)
            xc[tile(t0 + n - 1), :] = jnp.where(keep, xt, 0.0).astype(BF)
            sc[tile(t0 + n - 1), :] = jnp.where(keep, st, 0.0).astype(BF)

        def blank(t, _):
            xc[tile(t), :] = zeros
            sc[tile(t), :] = zeros
            return 0

        lax.fori_loop(ends[2 * e], ends[2 * e + 1], blank, 0)
    for c in wcp:
        c.wait()
    nb0, nb = ends[1] // (BR // 16), ends[3] // (BR // 16)

    def out_copies(b):
        rows = pl.ds(pl.multiple_of(b * BR, BR), BR)
        return (pltpu.make_async_copy(pv.at[:, rows], part.at[:, rows], osem.at[0]),
                pltpu.make_async_copy(xc.at[rows], xc_o.at[rows], osem.at[1]),
                pltpu.make_async_copy(sc.at[rows], sc_o.at[rows], osem.at[2]))

    def block(b, _):
        e = (b >= nb0).astype(jnp.int32)
        rows = pl.ds(pl.multiple_of(b * BR, BR), BR)
        xb, sb = xc[rows, :], sc[rows, :]
        pv[0, rows, :] = jnp.dot(xb, wgv[e], preferred_element_type=F32).astype(BF)
        pv[1, rows, :] = jnp.dot(xb, wuv[e], preferred_element_type=F32).astype(BF)
        pv[2, rows, :] = lax.dot_general(
            sb, wdv[e], (((1,), (1,)), ((), ())), preferred_element_type=F32).astype(BF)
        for c in out_copies(b):
            c.start()
        return 0

    lax.fori_loop(0, nb, block, 0)

    def drain(b, _):
        for c in out_copies(b):
            c.wait()
        return 0

    lax.fori_loop(0, nb, drain, 0)


def first_matmuls(counts, xg, sg, wg, wu, wd):
    any_ = pl.BlockSpec(memory_space=pl.ANY)
    return pl.pallas_call(
        first_kernel,
        out_shape=(jax.ShapeDtypeStruct((3, RMAX, HID), BF),
                   jax.ShapeDtypeStruct((RMAX, DS), BF),
                   jax.ShapeDtypeStruct((RMAX, DS), BF)),
        in_specs=[pl.BlockSpec(memory_space=pltpu.SMEM)] + [any_] * 5,
        out_specs=(any_,) * 3,
        scratch_shapes=[
            pltpu.VMEM((ROWS, DS), BF), pltpu.VMEM((ROWS, DS), BF),
            pltpu.VMEM((RMAX, DS), BF), pltpu.VMEM((RMAX, DS), BF),
            pltpu.VMEM((2, DS, HID), BF), pltpu.VMEM((2, DS, HID), BF), pltpu.VMEM((2, HID, DS), BF),
            pltpu.VMEM((3, RMAX, HID), BF),
            pltpu.SemaphoreType.DMA((2, 32)), pltpu.SemaphoreType.DMA((3,)),
            pltpu.SemaphoreType.DMA((3,)),
        ],
        compiler_params=pltpu.CompilerParams(vmem_limit_bytes=VLIM),
        name="first_matmuls",
    )(counts, xg, sg, wg, wu, wd)


def exchange_kernel(r, p, h, own, prt, q, l1, r1, s1, s2, l2, r2, res,
                    osem, psend, precv, bsend, brecv, gsend, grecv, lsem):
    d = lax.axis_index("dp")
    z, c = d // 2, d % 2
    r8, r16 = r // 8, r // 16
    up, down = {"dp": (z + 1) % 4 * 2 + c}, {"dp": (z + 3) % 4 * 2 + c}
    mate = {"dp": z * 2 + 1 - c}
    greet([up, down, mate])

    def rows(zz, cc):
        return pl.ds(pl.multiple_of((zz % 4 * 2 + cc) * r8, r16), r8)

    def half(zz, cc, i):
        return pl.ds(pl.multiple_of((zz % 4 * 2 + cc) * r8 + i * r16, r16), r16)

    first, second = pl.ds(0, r16), pl.ds(r16, r16)
    order = (2, 1, 3, 0)
    pair, mine = {}, {}
    for i in order:
        pair[i] = rcopy(p.at[:, rows(z + i, 1 - c)], prt.at[i], psend.at[i], precv.at[i], mate)
        pair[i].start()
        mine[i] = pltpu.make_async_copy(p.at[:, rows(z + i, c)], own.at[i], osem.at[i])
        mine[i].start()

    def bsum(i):
        mine[i].wait()
        pair[i].wait_recv()
        for k in range(3):
            q[i, k] = (own[i, k].astype(F32) + prt[i, k].astype(F32)).astype(BF)

    cps = []

    def push(i, src, dst, dev):
        cp = rcopy(src, dst, bsend.at[i], brecv.at[i], dev)
        cp.start()
        cps.append(cp)
        return cp

    bsum(2)
    a_l = push(0, q.at[2, :, first], l1, up)
    a_r = push(1, q.at[2, :, second], r1, down)
    bsum(1)
    b_l2 = push(2, q.at[1, :, second], l2.at[:, second], up)
    bsum(3)
    b_r1 = push(3, q.at[3, :, first], r2.at[:, first], down)
    a_l.wait_recv()
    for k in range(3):
        s1[k] = (l1[k].astype(F32) + q[1, k, 0:r16].astype(F32)).astype(BF)
    b_l1 = push(4, s1, l2.at[:, first], up)
    a_r.wait_recv()
    for k in range(3):
        s2[k] = (r1[k].astype(F32) + q[3, k, r16:r8].astype(F32)).astype(BF)
    b_r2 = push(5, s2, r2.at[:, second], down)
    mine[0].wait()
    pair[0].wait_recv()
    for cp in (b_l2, b_r1, b_l1, b_r2):
        cp.wait_recv()

    def total(k):
        return (own[0, k].astype(F32) + prt[0, k].astype(F32)
                + l2[k].astype(F32) + r2[k].astype(F32))

    gate, lin, grad = total(0), total(1), total(2)
    s = 1.0 / (1.0 + jnp.exp(-gate))
    act = gate * s
    res[0] = (act * lin).astype(BF)
    res[1] = (grad * lin * s * (1.0 + gate * (1.0 - s))).astype(BF)
    res[2] = (grad * act).astype(BF)

    keep = pltpu.make_async_copy(res, h.at[:, rows(z, c)], lsem)
    keep.start()
    gps = {}

    def spread(i, src, dst, dev):
        cp = rcopy(src, dst, gsend.at[i], grecv.at[i], dev)
        cp.start()
        gps[i] = cp

    spread(0, res, h.at[:, rows(z, c)], up)
    spread(1, res, h.at[:, rows(z, c)], down)
    spread(2, res, h.at[:, rows(z, c)], mate)
    gps[0].wait_recv()
    spread(3, h.at[:, half(z + 3, c, 0)], h.at[:, half(z + 3, c, 0)], up)
    spread(4, h.at[:, rows(z + 3, c)], h.at[:, rows(z + 3, c)], mate)
    gps[1].wait_recv()
    spread(5, h.at[:, half(z + 1, c, 1)], h.at[:, half(z + 1, c, 1)], down)
    spread(6, h.at[:, rows(z + 1, c)], h.at[:, rows(z + 1, c)], mate)
    gps[3].wait_recv()
    spread(7, h.at[:, half(z + 2, c, 0)], h.at[:, half(z + 2, c, 0)], mate)
    gps[5].wait_recv()
    spread(8, h.at[:, half(z + 2, c, 1)], h.at[:, half(z + 2, c, 1)], mate)
    for i in (2, 4, 6, 7, 8):
        gps[i].wait_recv()
    keep.wait()
    for cp in list(pair.values()) + cps + list(gps.values()):
        cp.wait_send()


def exchange(r, cid, part):
    r8, r16 = r // 8, r // 16
    any_ = pl.BlockSpec(memory_space=pl.ANY)
    v = lambda *s: pltpu.VMEM(s, BF)
    dma = lambda n: pltpu.SemaphoreType.DMA((n,))
    return pl.pallas_call(
        functools.partial(exchange_kernel, r),
        out_shape=jax.ShapeDtypeStruct((3, RMAX, HID), BF),
        in_specs=[any_],
        out_specs=any_,
        scratch_shapes=[
            v(4, 3, r8, HID), v(4, 3, r8, HID), v(4, 3, r8, HID),
            v(3, r16, HID), v(3, r16, HID), v(3, r16, HID), v(3, r16, HID),
            v(3, r8, HID), v(3, r8, HID), v(3, r8, HID),
            dma(4), dma(4), dma(4), dma(6), dma(6), dma(9), dma(9), pltpu.SemaphoreType.DMA,
        ],
        compiler_params=pltpu.CompilerParams(
            collective_id=cid, has_side_effects=True, vmem_limit_bytes=VLIM),
        name="exchange_%d" % r,
    )(part)


def second_kernel(cnt, h, xc_i, sc_i, wg, wu, wd, o, gr, dg, du, dd,
                  hv, xc, sc, wgv, wuv, wdv, ov, gv, ag, au, ad, bsem, wsem):
    d = lax.axis_index("dp")
    cols = pl.ds(pl.multiple_of(d * DS, DS), DS)
    segs, ends = segments(cnt)
    nb0, nb = ends[1] // (BR // 16), ends[3] // (BR // 16)
    wcp = [pltpu.make_async_copy(wg.at[:, cols, :], wgv, wsem.at[0]),
           pltpu.make_async_copy(wu.at[:, cols, :], wuv, wsem.at[1]),
           pltpu.make_async_copy(wd.at[:, :, cols], wdv, wsem.at[2])]

    def in_copies(b):
        rows = pl.ds(pl.multiple_of(b * BR, BR), BR)
        return (pltpu.make_async_copy(h.at[:, rows], hv.at[:, rows], bsem.at[0, b]),
                pltpu.make_async_copy(xc_i.at[rows], xc.at[rows], bsem.at[1, b]),
                pltpu.make_async_copy(sc_i.at[rows], sc.at[rows], bsem.at[2, b]))

    for c in wcp:
        c.start()

    def begin(b, _):
        for c in in_copies(b):
            c.start()
        return 0

    lax.fori_loop(0, nb, begin, 0)
    ag[...] = jnp.zeros_like(ag)
    au[...] = jnp.zeros_like(au)
    ad[...] = jnp.zeros_like(ad)
    for c in wcp:
        c.wait()
    tr = (((1,), (1,)), ((), ()))
    tl = (((0,), (0,)), ((), ()))

    def block(b, _):
        e = (b >= nb0).astype(jnp.int32)
        rows = pl.ds(pl.multiple_of(b * BR, BR), BR)
        for c in in_copies(b):
            c.wait()
        hb, gb, lb = hv[0, rows, :], hv[1, rows, :], hv[2, rows, :]
        ov[rows, :] = jnp.dot(hb, wdv[e], preferred_element_type=F32).astype(BF)
        gv[rows, :] = (lax.dot_general(gb, wgv[e], tr, preferred_element_type=F32)
                       + lax.dot_general(lb, wuv[e], tr, preferred_element_type=F32)).astype(BF)
        xb, sb = xc[rows, :], sc[rows, :]
        ag[e] += lax.dot_general(xb, gb, tl, preferred_element_type=F32)
        au[e] += lax.dot_general(xb, lb, tl, preferred_element_type=F32)
        ad[e] += lax.dot_general(hb, sb, tl, preferred_element_type=F32)
        return 0

    lax.fori_loop(0, nb, block, 0)
    dg[...] = ag[...].astype(BF)
    du[...] = au[...].astype(BF)
    dd[...] = ad[...].astype(BF)

    zeros = jnp.zeros((16, DS), BF)
    for g in range(GROUPS):
        base = g * (SLOTS // 16)
        stop = SLOTS // 16
        for e in (1, 0):
            c, first, n, t0 = segs[e][g]
            s0 = first // 16

            def move(k, _, base=base, s0=s0, t0=t0):
                o[tile(base + s0 + k), :] = ov[tile(t0 + k), :]
                gr[tile(base + s0 + k), :] = gv[tile(t0 + k), :]
                return 0

            def blank(k, _, base=base):
                o[tile(base + k), :] = zeros
                gr[tile(base + k), :] = zeros
                return 0

            lax.fori_loop(0, n, move, 0)
            lax.fori_loop(s0 + n, stop, blank, 0)
            stop = s0


def second_matmuls(counts, h, xc, sc, wg, wu, wd):
    any_ = pl.BlockSpec(memory_space=pl.ANY)
    vm = pl.BlockSpec(memory_space=pltpu.VMEM)
    s = jax.ShapeDtypeStruct
    return pl.pallas_call(
        second_kernel,
        out_shape=(s((ROWS, DS), BF), s((ROWS, DS), BF),
                   s((2, DS, HID), BF), s((2, DS, HID), BF), s((2, HID, DS), BF)),
        in_specs=[pl.BlockSpec(memory_space=pltpu.SMEM)] + [any_] * 6,
        out_specs=(vm,) * 5,
        scratch_shapes=[
            pltpu.VMEM((3, RMAX, HID), BF),
            pltpu.VMEM((RMAX, DS), BF), pltpu.VMEM((RMAX, DS), BF),
            pltpu.VMEM((2, DS, HID), BF), pltpu.VMEM((2, DS, HID), BF), pltpu.VMEM((2, HID, DS), BF),
            pltpu.VMEM((RMAX, DS), BF), pltpu.VMEM((RMAX, DS), BF),
            pltpu.VMEM((2, DS, HID), F32), pltpu.VMEM((2, DS, HID), F32), pltpu.VMEM((2, HID, DS), F32),
            pltpu.SemaphoreType.DMA((3, RMAX // BR)), pltpu.SemaphoreType.DMA((3,)),
        ],
        compiler_params=pltpu.CompilerParams(vmem_limit_bytes=VLIM),
        name="second_matmuls",
    )(counts, h, xc, sc, wg, wu, wd)


def reduce_kernel(o_ref, g_ref, rw_ref, oc_ref, out_o, out_w, out_g,
                  l1, r1, s1, s2, l2, r2, acc, bl1, br1, bs1, bs2, bl2, br2, fin, rec,
                  asend, arecv, bsend, brecv, psend, precv):
    d, j = lax.axis_index("dp"), lax.axis_index("et")
    y, x = j // 4, j % 4
    greet([{"dp": (d + k) % 8} for k in range(1, 8)]
          + [plane("x", x + 1, j), plane("x", x + 3, j), plane("y", y + 1, j), plane("y", y + 3, j)])
    lo, hi = pl.ds(0, 4), pl.ds(4, 4)
    order = (2, 1, 3, 0)
    info = []
    cps = []
    for a, (src, first) in enumerate(((o_ref, "y"), (g_ref, "x"))):
        second = "x" if first == "y" else "y"
        p, q = (y, x) if first == "y" else (x, y)

        def blk(pp, qq, g, src=src, first=first):
            yy, xx = (pp % 4, qq % 4) if first == "y" else (qq % 4, pp % 4)
            return src.at[g, yy, xx]

        info.append((p, q, first, second, blk))

    def push(sems, key, src, dst, axis, pos):
        send, recv = sems
        cp = rcopy(src, dst, send.at[key], recv.at[key], plane(axis, pos, j))
        cp.start()
        cps.append(cp)
        return cp

    def add2(dst, b, c):
        for g in range(4):
            dst[g] = (b[g].astype(F32) + c[g].astype(F32)).astype(BF)

    A, B = (asend, arecv), (bsend, brecv)
    av = [dict(), dict()]
    for u in order:
        for a in range(2):
            p, q, first, second, blk = info[a]
            av[a][u, 0] = push(A, (a, u, 0), blk(p + 2, q + u, lo), l1.at[a, u], first, p + 1)
            av[a][u, 1] = push(A, (a, u, 1), blk(p + 2, q + u, hi), r1.at[a, u], first, p + 3)
            av[a][u, 2] = push(A, (a, u, 2), blk(p + 1, q + u, hi), l2.at[a, u, hi], first, p + 1)
            av[a][u, 3] = push(A, (a, u, 3), blk(p + 3, q + u, lo), r2.at[a, u, lo], first, p + 3)
    for u in order:
        for a in range(2):
            p, q, first, second, blk = info[a]
            av[a][u, 0].wait_recv()
            add2(s1.at[a, u], l1.at[a, u], blk(p + 1, q + u, lo))
            av[a][u, 4] = push(A, (a, u, 4), s1.at[a, u], l2.at[a, u, lo], first, p + 1)
            av[a][u, 1].wait_recv()
            add2(s2.at[a, u], r1.at[a, u], blk(p + 3, q + u, hi))
            av[a][u, 5] = push(A, (a, u, 5), s2.at[a, u], r2.at[a, u, hi], first, p + 3)
    bv = [dict(), dict()]
    for u in order:
        for a in range(2):
            p, q, first, second, blk = info[a]
            for i in (2, 3, 4, 5):
                av[a][u, i].wait_recv()
            mine = blk(p, q + u, pl.ds(0, 8))
            for g in range(8):
                acc[a, u, g] = (mine[g].astype(F32) + l2[a, u, g].astype(F32)
                                + r2[a, u, g].astype(F32)).astype(BF)
            if u == 2:
                bv[a][0] = push(B, (a, 0), acc.at[a, 2, lo], bl1.at[a], second, q + 1)
                bv[a][1] = push(B, (a, 1), acc.at[a, 2, hi], br1.at[a], second, q + 3)
            elif u == 1:
                bv[a][2] = push(B, (a, 2), acc.at[a, 1, hi], bl2.at[a, hi], second, q + 1)
            elif u == 3:
                bv[a][3] = push(B, (a, 3), acc.at[a, 3, lo], br2.at[a, lo], second, q + 3)
    for a in range(2):
        p, q, first, second, blk = info[a]
        bv[a][0].wait_recv()
        add2(bs1.at[a], bl1.at[a], acc.at[a, 1, lo])
        bv[a][4] = push(B, (a, 4), bs1.at[a], bl2.at[a, lo], second, q + 1)
        bv[a][1].wait_recv()
        add2(bs2.at[a], br1.at[a], acc.at[a, 3, hi])
        bv[a][5] = push(B, (a, 5), bs2.at[a], br2.at[a, hi], second, q + 3)
    pv = []
    for a in range(2):
        for i in (2, 3, 4, 5):
            bv[a][i].wait_recv()
        for g in range(8):
            fin[a, g] = (acc[a, 0, g].astype(F32) + bl2[a, g].astype(F32)
                         + br2[a, g].astype(F32)).astype(BF)
        for k in range(1, 8):
            g = (d + k) % 8
            cp = rcopy(fin.at[a, g], rec.at[a, d], psend.at[a, k - 1], precv.at[a, k - 1], {"dp": g})
            cp.start()
            cps.append(cp)
            pv.append(cp)
        rec[a, d] = fin[a, d]
    for cp in pv:
        cp.wait_recv()
    rw = rw_ref[...]
    total = jnp.zeros((OWN, 1), F32)
    for k in range(8):
        cols = slice(k * DS, (k + 1) * DS)
        comb = rec[0, k].astype(F32)
        out_o[:, cols] = (rw * comb).astype(BF)
        total = total + jnp.sum(oc_ref[:, cols].astype(F32) * comb, axis=1, keepdims=True)
        out_g[:, cols] = rec[1, k]
    out_w[...] = total
    for cp in cps:
        cp.wait_send()


def reduce_rows(o, g, rw, oc):
    vm = pl.BlockSpec(memory_space=pltpu.VMEM)
    s = jax.ShapeDtypeStruct
    v = lambda *sh: pltpu.VMEM(sh + (OWN, DS), BF)
    dma = lambda *n: pltpu.SemaphoreType.DMA(n)
    return pl.pallas_call(
        reduce_kernel,
        out_shape=(s((OWN, DM), BF), s((OWN, 1), F32), s((OWN, DM), BF)),
        in_specs=[vm] * 4,
        out_specs=(vm,) * 3,
        scratch_shapes=[
            v(2, 4, 4), v(2, 4, 4), v(2, 4, 4), v(2, 4, 4), v(2, 4, 8), v(2, 4, 8), v(2, 4, 8),
            v(2, 4), v(2, 4), v(2, 4), v(2, 4), v(2, 8), v(2, 8), v(2, 8), v(2, 8),
            dma(2, 4, 6), dma(2, 4, 6), dma(2, 6), dma(2, 6), dma(2, 7), dma(2, 7),
        ],
        compiler_params=pltpu.CompilerParams(
            collective_id=1, has_side_effects=True, vmem_limit_bytes=VLIM),
        name="reduce_rows",
    )(o.reshape(GROUPS, 4, 4, OWN, DS), g.reshape(GROUPS, 4, 4, OWN, DS), rw, oc)


def per_device(routed_rows, out_cotangent, route_weight, expert_counts, w_gate, w_up, w_down):
    rw = route_weight[:, None]
    scaled = (rw * out_cotangent.astype(F32)).astype(BF)
    tiles = jnp.sum((expert_counts + 15) // 16, axis=0)
    live = jnp.sum((tiles * 16 + BR - 1) // BR) * BR
    level = sum((live > r).astype(jnp.int32) for r in LEVELS[:-1])
    xg, sg = gather_rows(routed_rows, scaled)
    part, xc, sc = first_matmuls(expert_counts, xg.reshape(ROWS, DS), sg.reshape(ROWS, DS),
                                 w_gate, w_up, w_down)
    h = lax.switch(level, [functools.partial(exchange, r, 2 + i) for i, r in enumerate(LEVELS)], part)
    o, gr, dg, du, dd = second_matmuls(expert_counts, h, xc, sc, w_gate, w_up, w_down)
    layer_out, grad_weight, grad_rows = reduce_rows(o, gr, rw, out_cotangent)
    return (layer_out, grad_weight[:, 0], grad_rows, dg, du, dd)


def solution(mesh):
    return jax.shard_map(
        per_device,
        mesh=mesh,
        in_specs=(
            P(("dp", "et"), None),
            P(("dp", "et"), None),
            P(("dp", "et")),
            P(),
            P(None, None, "et"),
            P(None, None, "et"),
            P(None, "et", None),
        ),
        out_specs=(
            P(("dp", "et"), None),
            P(("dp", "et")),
            P(("dp", "et"), None),
            P(None, "dp", "et"),
            P(None, "dp", "et"),
            P(None, "et", "dp"),
        ),
        check_vma=False,
    )
```

```python
import functools

import jax
import jax.numpy as jnp
from jax import lax
from jax.experimental import pallas as pl
from jax.experimental.pallas import tpu as pltpu
from jax.sharding import PartitionSpec as P

MESH = pl.DeviceIdType.MESH
BF = jnp.bfloat16
F32 = jnp.float32
GROUPS, SLOTS, OWN, DM, HID = 8, 512, 32, 4096, 448
DS = DM // GROUPS
ROWS = GROUPS * SLOTS
H2, H3 = 2 * HID, 3 * HID
BR = 256
T = 16
TB = BR // T
PLANS = ((8, (1536, 1792, 2304)), (10, (2816,)), (16, (ROWS + BR,)))
VLIM = 60 * 1024 * 1024


def rcopy(src, dst, ssem, rsem, dev):
    return pltpu.make_async_remote_copy(
        src_ref=src, dst_ref=dst, send_sem=ssem, recv_sem=rsem,
        device_id=dev, device_id_type=MESH,
    )


def spot(g, s):
    return (s + 3 * g + 8 * (s // 16)) % 16


def origin(g, m, j):
    return 16 * m + (j + 32 - 3 * g - 8 * m) % 16


def plane(axis, pos, j):
    y, x = j // 4, j % 4
    return {"et": y * 4 + pos % 4} if axis == "x" else {"et": (pos % 4) * 4 + x}


def greet(near, others):
    bar = pltpu.get_barrier_semaphore()
    for dev in near:
        pl.semaphore_signal(bar, inc=1, device_id=dev, device_id_type=MESH)
    for dd, jj in others:
        pl.semaphore_signal(bar, inc=1, device_id={"dp": dd, "et": jj}, device_id_type=MESH)
    pl.semaphore_wait(bar, len(near) + len(others))


def deliver(me, src, dst, ssem, rsem, dd, jj):
    d, j = me
    here = jnp.logical_and(dd == d, jj == j)
    far = rcopy(src, dst, ssem, rsem, {"dp": dd, "et": jj})

    @pl.when(here)
    def _():
        pltpu.make_async_copy(src, dst, rsem).start()

    @pl.when(jnp.logical_not(here))
    def _():
        far.start()

    def finish():
        @pl.when(jnp.logical_not(here))
        def _():
            far.wait_send()

    return finish


def gather_kernel(cap, tab, rows_ref, oc_ref, rw_ref, xg, sg,
                  sc, rb0, rb1, stage, psend, precv, osem, rsend, rrecv):
    d, j = lax.axis_index("dp"), lax.axis_index("et")
    me = (d, j)
    y, x = j // 4, j % 4
    lo = cap // 2
    senders = [((d + 8 - k) % 8, origin((d + 8 - k) % 8, m, j) // 2) for k in range(8) for m in range(2)]
    greet([plane("x", x + 1, j), plane("x", x + 3, j), plane("y", y + 1, j), plane("y", y + 3, j)],
          senders)
    mm = j // 8
    rb = (rb0, rb1)
    done = []
    arrays = []
    for a, (src, out, first, second) in enumerate(
        ((rows_ref, xg, "x", "y"), (sc, sg, "y", "x"))
    ):
        if a == 1:
            sc[...] = (rw_ref[...] * oc_ref[...].astype(F32)).astype(BF)
        for k in range(8):
            dd = (d + k) % 8
            cols = pl.ds(pl.multiple_of(dd * DS, DS), DS)
            for hh in range(2):
                jj = spot(d, 2 * j + hh)
                done.append(deliver(me, src.at[pl.ds(T * hh, T), cols], rb[a].at[2 * d + mm],
                                    psend.at[a, k, hh], precv.at[a, k, mm], dd, jj))
        p, q = (x, y) if first == "x" else (y, x)

        def blk(pp, qq, half=None, out=out, first=first):
            yy, xx = (qq % 4, pp % 4) if first == "x" else (pp % 4, qq % 4)
            g = slice(None) if half is None else (pl.ds(0, lo) if half == 0 else pl.ds(lo, cap - lo))
            return out.at[yy, xx, g]

        def send(i, ref, axis, pos, a=a, own=None):
            c = rcopy(ref if own is None else own, ref, rsend.at[a, i], rrecv.at[a, i], plane(axis, pos, j))
            c.start()
            return c

        arrays.append((p, q, first, second, blk, send))

    sent = [dict(), dict()]

    def second_sends(a, u, own=None):
        p, q, first, second, blk, send = arrays[a]
        base = 4 + 4 * (u % 4)
        sent[a][base] = send(base, blk(p + u, q), second, q + 1, own=own)
        sent[a][base + 1] = send(base + 1, blk(p + u, q), second, q + 3, own=own)

    def second_forward(a, u):
        p, q, first, second, blk, send = arrays[a]
        base = 4 + 4 * (u % 4)
        sent[a][base].wait_recv()
        sent[a][base + 2] = send(base + 2, blk(p + u, q + 3, 0), second, q + 1)
        sent[a][base + 1].wait_recv()
        sent[a][base + 3] = send(base + 3, blk(p + u, q + 1, 1), second, q + 3)

    keep = []
    for a in range(2):
        p, q, first, second, blk, send = arrays[a]
        for k in range(8):
            for m in range(2):
                g = (d + 8 - k) % 8
                pltpu.make_async_copy(rb[a].at[2 * g + m], rb[a].at[2 * g + m], precv.at[a, k, m]).wait()
        for i in range(cap):
            stage[a, i] = rb[a][tab[j, i]]
        sent[a][0] = send(0, blk(p, q), first, p + 1, own=stage.at[a])
        sent[a][1] = send(1, blk(p, q), first, p + 3, own=stage.at[a])
        second_sends(a, 0, own=stage.at[a])
        c = pltpu.make_async_copy(stage.at[a], blk(p, q), osem.at[a])
        c.start()
        keep.append(c)
    for a in range(2):
        p, q, first, second, blk, send = arrays[a]
        sent[a][0].wait_recv()
        sent[a][2] = send(2, blk(p + 3, q, 0), first, p + 1)
        second_sends(a, 3)
        sent[a][1].wait_recv()
        sent[a][3] = send(3, blk(p + 1, q, 1), first, p + 3)
        second_sends(a, 1)
    for a in range(2):
        second_forward(a, 0)
    for a in range(2):
        sent[a][2].wait_recv()
        sent[a][3].wait_recv()
        second_sends(a, 2)
    for u in (3, 1, 2):
        for a in range(2):
            second_forward(a, u)
    for a in range(2):
        keep[a].wait()
        for u in range(4):
            sent[a][6 + 4 * u].wait_recv()
            sent[a][7 + 4 * u].wait_recv()
        for c in sent[a].values():
            c.wait_send()
    for f in done:
        f()


def gather_rows(cap, cid, tab, rows, oc, rw):
    shape = jax.ShapeDtypeStruct((4, 4, cap, T, DS), BF)
    vm = pl.BlockSpec(memory_space=pltpu.VMEM)
    return pl.pallas_call(
        functools.partial(gather_kernel, cap),
        out_shape=(shape, shape),
        in_specs=[pl.BlockSpec(memory_space=pltpu.SMEM), vm, vm, vm],
        out_specs=(pl.BlockSpec(memory_space=pl.ANY),) * 2,
        scratch_shapes=[
            pltpu.VMEM((OWN, DM), BF),
            pltpu.VMEM((16, T, DS), BF),
            pltpu.VMEM((16, T, DS), BF),
            pltpu.VMEM((2, cap, T, DS), BF),
            pltpu.SemaphoreType.DMA((2, 8, 2)),
            pltpu.SemaphoreType.DMA((2, 8, 2)),
            pltpu.SemaphoreType.DMA((2,)),
            pltpu.SemaphoreType.DMA((2, 20)),
            pltpu.SemaphoreType.DMA((2, 20)),
        ],
        compiler_params=pltpu.CompilerParams(
            collective_id=cid, has_side_effects=True, vmem_limit_bytes=VLIM),
        name="gather_rows_%d" % cap,
    )(tab, rows, oc, rw)


def segments(cnt):
    segs, t = [], 0
    ends = []
    for e in range(2):
        row = []
        for g in range(GROUPS):
            c = cnt[g, e]
            first = 0 if e == 0 else (cnt[g, 0] + 127) // 128 * 8
            n = (c + T - 1) // T
            row.append((c, first, n, t))
            t = t + n
        ends.append(t)
        t = (t + TB - 1) // TB * TB
        ends.append(t)
        segs.append(row)
    return segs, ends


def tile(i):
    return pl.ds(pl.multiple_of(i * T, T), T)


def rows_of(b):
    return pl.ds(pl.multiple_of(b * BR, BR), BR)


def weight_copies(wg, wu, wd, wb, wsem):
    d = lax.axis_index("dp")
    cols = pl.ds(pl.multiple_of(d * DS, DS), DS)
    return [pltpu.make_async_copy(w.at[:, :, cols], wb.at[:, pl.ds(i * HID, HID), :], wsem.at[i])
            for i, w in enumerate((wg, wu, wd))]


TRANS_R = (((1,), (1,)), ((), ()))
TRANS_L = (((0,), (0,)), ((), ()))


def first_kernel(cap, cnt, tab, xg, sg, wg, wu, wd, part, xc_o, sc_o,
                 xv, sv, xc, sc, wb, pv, rsem, wsem, osem):
    segs, ends = segments(cnt)
    loads = [pltpu.make_async_copy(xg, xv, rsem.at[0]), pltpu.make_async_copy(sg, sv, rsem.at[1])]
    wcp = weight_copies(wg, wu, wd, wb, wsem)
    for c in loads + wcp:
        c.start()
    for c in loads:
        c.wait()
    zeros = jnp.zeros((T, DS), BF)
    iota = lax.broadcasted_iota(jnp.int32, (T, DS), 0)

    def source(g, s):
        jj = spot(g, s)
        return tile(jj * cap + tab[16 + jj, 2 * g + s // 16])

    for e in range(2):
        for g in range(GROUPS):
            c, first, n, t0 = segs[e][g]

            def move(k, _, g=g, first=first, t0=t0):
                src = source(g, first + k)
                xc[tile(t0 + k), :] = xv[src, :]
                sc[tile(t0 + k), :] = sv[src, :]
                return 0

            lax.fori_loop(0, n - 1, move, 0)
            keep = iota < c - T * (n - 1)
            src = source(g, first + n - 1)
            xt = xv[src, :].astype(F32)
            st = sv[src, :].astype(F32)
            xc[tile(t0 + n - 1), :] = jnp.where(keep, xt, 0.0).astype(BF)
            sc[tile(t0 + n - 1), :] = jnp.where(keep, st, 0.0).astype(BF)

        def blank(t, _):
            xc[tile(t), :] = zeros
            sc[tile(t), :] = zeros
            return 0

        lax.fori_loop(ends[2 * e], ends[2 * e + 1], blank, 0)
    for c in wcp:
        c.wait()
    nb0, nb = ends[1] // TB, ends[3] // TB

    def out_copies(b):
        rows = rows_of(b)
        return (pltpu.make_async_copy(pv.at[rows], part.at[rows], osem.at[0]),
                pltpu.make_async_copy(xc.at[rows], xc_o.at[rows], osem.at[1]),
                pltpu.make_async_copy(sc.at[rows], sc_o.at[rows], osem.at[2]))

    def block(b, _):
        e = (b >= nb0).astype(jnp.int32)
        rows = rows_of(b)
        pv[rows, 0:H2] = lax.dot_general(
            xc[rows, :], wb[e, 0:H2, :], TRANS_R, preferred_element_type=F32).astype(BF)
        pv[rows, H2:H3] = lax.dot_general(
            sc[rows, :], wb[e, H2:H3, :], TRANS_R, preferred_element_type=F32).astype(BF)
        for c in out_copies(b):
            c.start()
        return 0

    lax.fori_loop(0, nb, block, 0)

    def drain(b, _):
        for c in out_copies(b):
            c.wait()
        return 0

    lax.fori_loop(0, nb, drain, 0)


def first_matmuls(cap, rmax, counts, tab, xg, sg, wg, wu, wd):
    any_ = pl.BlockSpec(memory_space=pl.ANY)
    sm = pl.BlockSpec(memory_space=pltpu.SMEM)
    n = 16 * cap * T
    return pl.pallas_call(
        functools.partial(first_kernel, cap),
        out_shape=(jax.ShapeDtypeStruct((rmax, H3), BF),
                   jax.ShapeDtypeStruct((rmax, DS), BF),
                   jax.ShapeDtypeStruct((rmax, DS), BF)),
        in_specs=[sm, sm] + [any_] * 5,
        out_specs=(any_,) * 3,
        scratch_shapes=[
            pltpu.VMEM((n, DS), BF), pltpu.VMEM((n, DS), BF),
            pltpu.VMEM((rmax, DS), BF), pltpu.VMEM((rmax, DS), BF),
            pltpu.VMEM((2, H3, DS), BF),
            pltpu.VMEM((rmax, H3), BF),
            pltpu.SemaphoreType.DMA((2,)), pltpu.SemaphoreType.DMA((3,)),
            pltpu.SemaphoreType.DMA((3,)),
        ],
        compiler_params=pltpu.CompilerParams(vmem_limit_bytes=VLIM),
        name="first_matmuls_%d" % cap,
    )(counts, tab, xg.reshape(n, DS), sg.reshape(n, DS), wg, wu, wd)


def exchange_kernel(r, p, h, own, prt, q, l1, r1, s1, s2, l2, r2, tot, res,
                    osem, psend, precv, bsend, brecv, gsend, grecv, lsem):
    d = lax.axis_index("dp")
    z, c = d // 2, d % 2
    r8, r16 = r // 8, r // 16
    up, down = {"dp": (z + 1) % 4 * 2 + c}, {"dp": (z + 3) % 4 * 2 + c}
    mate = {"dp": z * 2 + 1 - c}
    bar = pltpu.get_barrier_semaphore()
    for dev in (up, down, mate):
        pl.semaphore_signal(bar, inc=1, device_id=dev, device_id_type=MESH)
    pl.semaphore_wait(bar, 3)

    def rows(zz, cc):
        return pl.ds(pl.multiple_of((zz % 4 * 2 + cc) * r8, r16), r8)

    def half(zz, cc, i):
        return pl.ds(pl.multiple_of((zz % 4 * 2 + cc) * r8 + i * r16, r16), r16)

    first, second = pl.ds(0, r16), pl.ds(r16, r16)
    pair, mine = {}, {}
    for i in (2, 1, 3, 0):
        pair[i] = rcopy(p.at[rows(z + i, 1 - c)], prt.at[i], psend.at[i], precv.at[i], mate)
        pair[i].start()
        mine[i] = pltpu.make_async_copy(p.at[rows(z + i, c)], own.at[i], osem.at[i])
        mine[i].start()

    def bsum(i):
        mine[i].wait()
        pair[i].wait_recv()

        def one(k, _):
            q[i, tile(k), :] = (own[i, tile(k), :].astype(F32) + prt[i, tile(k), :].astype(F32)).astype(BF)
            return 0

        lax.fori_loop(0, r8 // T, one, 0)

    def add_rows(dst, src, i, off):
        def one(k, _):
            dst[tile(k), :] = (src[tile(k), :].astype(F32) + q[i, tile(off + k), :].astype(F32)).astype(BF)
            return 0

        lax.fori_loop(0, r16 // T, one, 0)

    cps = []

    def push(i, src, dst, dev):
        cp = rcopy(src, dst, bsend.at[i], brecv.at[i], dev)
        cp.start()
        cps.append(cp)
        return cp

    bsum(2)
    a_l = push(0, q.at[2, first], l1, up)
    a_r = push(1, q.at[2, second], r1, down)
    bsum(1)
    b_l2 = push(2, q.at[1, second], l2.at[second], up)
    bsum(3)
    b_r1 = push(3, q.at[3, first], r2.at[first], down)
    a_l.wait_recv()
    add_rows(s1, l1, 1, 0)
    b_l1 = push(4, s1, l2.at[first], up)
    a_r.wait_recv()
    add_rows(s2, r1, 3, r16 // T)
    b_r2 = push(5, s2, r2.at[second], down)
    mine[0].wait()
    pair[0].wait_recv()
    for cp in (b_l2, b_r1, b_l1, b_r2):
        cp.wait_recv()

    def final(k, _):
        t = tile(k)
        tot[...] = (own[0, t, :].astype(F32) + prt[0, t, :].astype(F32)
                    + l2[t, :].astype(F32) + r2[t, :].astype(F32))
        gate, lin, grad = tot[:, 0:HID], tot[:, HID:H2], tot[:, H2:H3]
        s = 1.0 / (1.0 + jnp.exp(-gate))
        act = gate * s
        res[t, 0:HID] = (grad * lin * s * (1.0 + gate * (1.0 - s))).astype(BF)
        res[t, HID:H2] = (grad * act).astype(BF)
        res[t, H2:H3] = (act * lin).astype(BF)
        return 0

    lax.fori_loop(0, r8 // T, final, 0)
    keep = pltpu.make_async_copy(res, h.at[rows(z, c)], lsem)
    keep.start()
    gps = {}

    def spread(i, src, dst, dev):
        cp = rcopy(src, dst, gsend.at[i], grecv.at[i], dev)
        cp.start()
        gps[i] = cp

    spread(0, res, h.at[rows(z, c)], up)
    spread(1, res, h.at[rows(z, c)], down)
    spread(2, res, h.at[rows(z, c)], mate)
    gps[0].wait_recv()
    spread(3, h.at[half(z + 3, c, 0)], h.at[half(z + 3, c, 0)], up)
    spread(4, h.at[rows(z + 3, c)], h.at[rows(z + 3, c)], mate)
    gps[1].wait_recv()
    spread(5, h.at[half(z + 1, c, 1)], h.at[half(z + 1, c, 1)], down)
    spread(6, h.at[rows(z + 1, c)], h.at[rows(z + 1, c)], mate)
    gps[3].wait_recv()
    spread(7, h.at[half(z + 2, c, 0)], h.at[half(z + 2, c, 0)], mate)
    gps[5].wait_recv()
    spread(8, h.at[half(z + 2, c, 1)], h.at[half(z + 2, c, 1)], mate)
    for i in (2, 4, 6, 7, 8):
        gps[i].wait_recv()
    keep.wait()
    for cp in list(pair.values()) + cps + list(gps.values()):
        cp.wait_send()


def exchange(r, rmax, cid, part):
    r8, r16 = r // 8, r // 16
    any_ = pl.BlockSpec(memory_space=pl.ANY)
    v = lambda *s: pltpu.VMEM(s + (H3,), BF)
    dma = lambda n: pltpu.SemaphoreType.DMA((n,))
    return pl.pallas_call(
        functools.partial(exchange_kernel, r),
        out_shape=jax.ShapeDtypeStruct((rmax, H3), BF),
        in_specs=[any_],
        out_specs=any_,
        scratch_shapes=[
            v(4, r8), v(4, r8), v(4, r8),
            v(r16), v(r16), v(r16), v(r16),
            v(r8), v(r8), pltpu.VMEM((T, H3), F32), v(r8),
            dma(4), dma(4), dma(4), dma(6), dma(6), dma(9), dma(9), pltpu.SemaphoreType.DMA,
        ],
        compiler_params=pltpu.CompilerParams(
            collective_id=cid, has_side_effects=True, vmem_limit_bytes=VLIM),
        name="exchange_%d_%d" % (cid, r),
    )(part)


def second_kernel(cap, cnt, tab, h, xc_i, sc_i, wg, wu, wd, o, gr, dg, du, dd,
                  hv, xc, sc, wb, ov, gv, au, ad, bsem, wsem):
    segs, ends = segments(cnt)
    nb0, nb = ends[1] // TB, ends[3] // TB
    wcp = weight_copies(wg, wu, wd, wb, wsem)

    def in_copies(b):
        rows = rows_of(b)
        return (pltpu.make_async_copy(h.at[rows], hv.at[rows], bsem.at[0, b]),
                pltpu.make_async_copy(xc_i.at[rows], xc.at[rows], bsem.at[1, b]),
                pltpu.make_async_copy(sc_i.at[rows], sc.at[rows], bsem.at[2, b]))

    for c in wcp:
        c.start()

    def begin(b, _):
        for c in in_copies(b):
            c.start()
        return 0

    lax.fori_loop(0, nb, begin, 0)
    au[...] = jnp.zeros_like(au)
    ad[...] = jnp.zeros_like(ad)
    for c in wcp:
        c.wait()

    def block(b, _):
        e = (b >= nb0).astype(jnp.int32)
        rows = rows_of(b)
        for c in in_copies(b):
            c.wait()
        ov[rows, :] = jnp.dot(hv[rows, H2:H3], wb[e, H2:H3, :], preferred_element_type=F32).astype(BF)
        gv[rows, :] = jnp.dot(hv[rows, 0:H2], wb[e, 0:H2, :], preferred_element_type=F32).astype(BF)
        au[e] += lax.dot_general(hv[rows, 0:H2], xc[rows, :], TRANS_L, preferred_element_type=F32)
        ad[e] += lax.dot_general(hv[rows, H2:H3], sc[rows, :], TRANS_L, preferred_element_type=F32)
        return 0

    lax.fori_loop(0, nb, block, 0)
    dg[...] = au[:, 0:HID, :].astype(BF)
    du[...] = au[:, HID:H2, :].astype(BF)
    dd[...] = ad[...].astype(BF)

    for e in range(2):
        for g in range(GROUPS):
            c, first, n, t0 = segs[e][g]

            def move(k, _, g=g, first=first, t0=t0):
                s = first + k
                jj = spot(g, s)
                dst = tile(jj * cap + tab[16 + jj, 2 * g + s // 16])
                o[dst, :] = ov[tile(t0 + k), :]
                gr[dst, :] = gv[tile(t0 + k), :]
                return 0

            lax.fori_loop(0, n, move, 0)


def second_matmuls(cap, rmax, counts, tab, h, xc, sc, wg, wu, wd):
    any_ = pl.BlockSpec(memory_space=pl.ANY)
    sm = pl.BlockSpec(memory_space=pltpu.SMEM)
    vm = pl.BlockSpec(memory_space=pltpu.VMEM)
    s = jax.ShapeDtypeStruct
    n = 16 * cap * T
    return pl.pallas_call(
        functools.partial(second_kernel, cap),
        out_shape=(s((n, DS), BF), s((n, DS), BF)) + (s((2, HID, DS), BF),) * 3,
        in_specs=[sm, sm] + [any_] * 6,
        out_specs=(vm,) * 5,
        scratch_shapes=[
            pltpu.VMEM((rmax, H3), BF),
            pltpu.VMEM((rmax, DS), BF), pltpu.VMEM((rmax, DS), BF),
            pltpu.VMEM((2, H3, DS), BF),
            pltpu.VMEM((rmax, DS), BF), pltpu.VMEM((rmax, DS), BF),
            pltpu.VMEM((2, H2, DS), F32), pltpu.VMEM((2, HID, DS), F32),
            pltpu.SemaphoreType.DMA((3, rmax // BR)), pltpu.SemaphoreType.DMA((3,)),
        ],
        compiler_params=pltpu.CompilerParams(vmem_limit_bytes=VLIM),
        name="second_matmuls_%d" % cap,
    )(counts, tab, h, xc, sc, wg, wu, wd)


def reduce_kernel(cap, tab, o_ref, g_ref, rw_ref, oc_ref, out_o, out_w, out_g,
                  l1, r1, s1, s2, l2, r2, acc, bl1, br1, bs1, bs2, bl2, br2, fin, ex, rec,
                  asend, arecv, bsend, brecv, psend, precv):
    d, j = lax.axis_index("dp"), lax.axis_index("et")
    me = (d, j)
    y, x = j // 4, j % 4
    owners = [((d + k) % 8, spot(d, 2 * j + hh)) for k in range(8) for hh in range(2)]
    greet([plane("x", x + 1, j), plane("x", x + 3, j), plane("y", y + 1, j), plane("y", y + 3, j)],
          owners)
    half = cap // 2
    lo, hi = pl.ds(0, half), pl.ds(half, cap - half)
    order = (2, 1, 3, 0)
    info = []
    cps = []
    for a, (src, first) in enumerate(((o_ref, "y"), (g_ref, "x"))):
        second = "x" if first == "y" else "y"
        p, q = (y, x) if first == "y" else (x, y)

        def blk(pp, qq, g, src=src, first=first):
            yy, xx = (pp % 4, qq % 4) if first == "y" else (qq % 4, pp % 4)
            return src.at[yy, xx, g]

        info.append((p, q, first, second, blk))

    def push(sems, key, src, dst, axis, pos):
        send, recv = sems
        cp = rcopy(src, dst, send.at[key], recv.at[key], plane(axis, pos, j))
        cp.start()
        cps.append(cp)
        return cp

    def add2(dst, b, c):
        for g in range(half):
            dst[g] = (b[g].astype(F32) + c[g].astype(F32)).astype(BF)

    A, B = (asend, arecv), (bsend, brecv)
    av = [dict(), dict()]
    for u in order:
        for a in range(2):
            p, q, first, second, blk = info[a]
            av[a][u, 0] = push(A, (a, u, 0), blk(p + 2, q + u, lo), l1.at[a, u], first, p + 1)
            av[a][u, 1] = push(A, (a, u, 1), blk(p + 2, q + u, hi), r1.at[a, u], first, p + 3)
            av[a][u, 2] = push(A, (a, u, 2), blk(p + 1, q + u, hi), l2.at[a, u, hi], first, p + 1)
            av[a][u, 3] = push(A, (a, u, 3), blk(p + 3, q + u, lo), r2.at[a, u, lo], first, p + 3)
    for u in order:
        for a in range(2):
            p, q, first, second, blk = info[a]
            av[a][u, 0].wait_recv()
            add2(s1.at[a, u], l1.at[a, u], blk(p + 1, q + u, lo))
            av[a][u, 4] = push(A, (a, u, 4), s1.at[a, u], l2.at[a, u, lo], first, p + 1)
            av[a][u, 1].wait_recv()
            add2(s2.at[a, u], r1.at[a, u], blk(p + 3, q + u, hi))
            av[a][u, 5] = push(A, (a, u, 5), s2.at[a, u], r2.at[a, u, hi], first, p + 3)
    bv = [dict(), dict()]
    for u in order:
        for a in range(2):
            p, q, first, second, blk = info[a]
            for i in (2, 3, 4, 5):
                av[a][u, i].wait_recv()
            mine = blk(p, q + u, pl.ds(0, cap))
            for g in range(cap):
                acc[a, u, g] = (mine[g].astype(F32) + l2[a, u, g].astype(F32)
                                + r2[a, u, g].astype(F32)).astype(BF)
            if u == 2:
                bv[a][0] = push(B, (a, 0), acc.at[a, 2, lo], bl1.at[a], second, q + 1)
                bv[a][1] = push(B, (a, 1), acc.at[a, 2, hi], br1.at[a], second, q + 3)
            elif u == 1:
                bv[a][2] = push(B, (a, 2), acc.at[a, 1, hi], bl2.at[a, hi], second, q + 1)
            elif u == 3:
                bv[a][3] = push(B, (a, 3), acc.at[a, 3, lo], br2.at[a, lo], second, q + 3)
    for a in range(2):
        p, q, first, second, blk = info[a]
        bv[a][0].wait_recv()
        add2(bs1.at[a], bl1.at[a], acc.at[a, 1, lo])
        bv[a][4] = push(B, (a, 4), bs1.at[a], bl2.at[a, lo], second, q + 1)
        bv[a][1].wait_recv()
        add2(bs2.at[a], br1.at[a], acc.at[a, 3, hi])
        bv[a][5] = push(B, (a, 5), bs2.at[a], br2.at[a, hi], second, q + 3)
    done = []
    for a in range(2):
        for i in (2, 3, 4, 5):
            bv[a][i].wait_recv()
        for g in range(cap):
            fin[a, g] = (acc[a, 0, g].astype(F32) + bl2[a, g].astype(F32)
                         + br2[a, g].astype(F32)).astype(BF)
        for k in range(8):
            g = (d + k) % 8
            for m in range(2):
                s = origin(g, m, j)
                at = tab[16 + j, 2 * g + m]
                got = fin[a, jnp.maximum(at, 0)].astype(F32)
                ex[a, k, m] = jnp.where(at >= 0, got, 0.0).astype(BF)
                done.append(deliver(me, ex.at[a, k, m], rec.at[a, d, s % 2],
                                    psend.at[a, k, m], precv.at[a, k, s % 2], g, s // 2))
    for a in range(2):
        for k in range(8):
            for hh in range(2):
                spot_ref = rec.at[a, (d + 8 - k) % 8, hh]
                pltpu.make_async_copy(spot_ref, spot_ref, precv.at[a, k, hh]).wait()
    rw = rw_ref[...]
    total = jnp.zeros((OWN, 1), F32)
    for k in range(8):
        cols = slice(k * DS, (k + 1) * DS)
        comb = rec[0, k].astype(F32).reshape(OWN, DS)
        out_o[:, cols] = (rw * comb).astype(BF)
        total = total + jnp.sum(oc_ref[:, cols].astype(F32) * comb, axis=1, keepdims=True)
        out_g[:, cols] = rec[1, k].reshape(OWN, DS)
    out_w[...] = total
    for cp in cps:
        cp.wait_send()
    for f in done:
        f()


def reduce_rows(cap, cid, tab, o, g, rw, oc):
    vm = pl.BlockSpec(memory_space=pltpu.VMEM)
    s = jax.ShapeDtypeStruct
    v = lambda *sh: pltpu.VMEM(sh + (T, DS), BF)
    dma = lambda *n: pltpu.SemaphoreType.DMA(n)
    h = cap // 2
    return pl.pallas_call(
        functools.partial(reduce_kernel, cap),
        out_shape=(s((OWN, DM), BF), s((OWN, 1), F32), s((OWN, DM), BF)),
        in_specs=[pl.BlockSpec(memory_space=pltpu.SMEM)] + [vm] * 4,
        out_specs=(vm,) * 3,
        scratch_shapes=[
            v(2, 4, h), v(2, 4, h), v(2, 4, h), v(2, 4, h), v(2, 4, cap), v(2, 4, cap), v(2, 4, cap),
            v(2, h), v(2, h), v(2, h), v(2, h), v(2, cap), v(2, cap), v(2, cap),
            v(2, 8, 2), v(2, 8, 2),
            dma(2, 4, 6), dma(2, 4, 6), dma(2, 6), dma(2, 6), dma(2, 8, 2), dma(2, 8, 2),
        ],
        compiler_params=pltpu.CompilerParams(
            collective_id=cid, has_side_effects=True, vmem_limit_bytes=VLIM),
        name="reduce_rows_%d" % cap,
    )(tab, o.reshape(4, 4, cap, T, DS), g.reshape(4, 4, cap, T, DS), rw, oc)


def tile_tables(counts):
    j = lax.broadcasted_iota(jnp.int32, (16, 16), 0)
    q = lax.broadcasted_iota(jnp.int32, (16, 16), 1)
    g, m = q // 2, q % 2
    s = origin(g, m, j)
    c = jnp.repeat(counts, 2, axis=0)
    n0, n1 = (c[:, 0] + T - 1) // T, (c[:, 1] + T - 1) // T
    s1 = (c[:, 0] + 127) // 128 * 8
    live = (s < n0) | ((s >= s1) & (s < s1 + n1))
    one = live.astype(jnp.int32)
    rank = jnp.sum(jnp.where(q[:, None, :] < q[:, :, None], one[:, None, :], 0), axis=2)
    place = jnp.where(live, rank, -1)
    order = jnp.sum(jnp.where(place[:, None, :] == q[:, :, None], q[:, None, :], 0), axis=2)
    return jnp.concatenate([order, place], axis=0), jnp.max(jnp.sum(one, axis=1))


def run(cap, levels, cid, rows, oc, rw, counts, tab, live, wg, wu, wd):
    rmax = levels[-1]
    xg, sg = gather_rows(cap, cid, tab, rows, oc, rw)
    part, xc, sc = first_matmuls(cap, rmax, counts, tab, xg, sg, wg, wu, wd)
    level = sum((live > r).astype(jnp.int32) for r in levels[:-1])
    h = lax.switch(level, [functools.partial(exchange, r, rmax, cid + 2 + i)
                           for i, r in enumerate(levels)], part)
    o, gr, dg, du, dd = second_matmuls(cap, rmax, counts, tab, h, xc, sc, wg, wu, wd)
    layer_out, grad_weight, grad_rows = reduce_rows(cap, cid + 1, tab, o, gr, rw, oc)
    return layer_out, grad_weight, grad_rows, dg, du, dd


def per_device(routed_rows, out_cotangent, route_weight, expert_counts, w_gate, w_up, w_down):
    rw = route_weight[:, None]
    wg, wu = jnp.swapaxes(w_gate, 1, 2), jnp.swapaxes(w_up, 1, 2)
    tab, most = tile_tables(expert_counts)
    tiles = jnp.sum((expert_counts + T - 1) // T, axis=0)
    live = jnp.sum((tiles + TB - 1) // TB) * BR
    pick = sum((most > cap).astype(jnp.int32) for cap, _ in PLANS[:-1])
    branches = [functools.partial(run, cap, levels, 8 * i) for i, (cap, levels) in enumerate(PLANS)]
    layer_out, grad_weight, grad_rows, dg, du, dd = lax.switch(
        pick, branches, routed_rows, out_cotangent, rw, expert_counts, tab, live, wg, wu, w_down)
    return (layer_out, grad_weight[:, 0], grad_rows,
            jnp.swapaxes(dg, 1, 2), jnp.swapaxes(du, 1, 2), dd)


def solution(mesh):
    return jax.shard_map(
        per_device,
        mesh=mesh,
        in_specs=(
            P(("dp", "et"), None),
            P(("dp", "et"), None),
            P(("dp", "et")),
            P(),
            P(None, None, "et"),
            P(None, None, "et"),
            P(None, "et", None),
        ),
        out_specs=(
            P(("dp", "et"), None),
            P(("dp", "et")),
            P(("dp", "et"), None),
            P(None, "dp", "et"),
            P(None, "dp", "et"),
            P(None, "et", "dp"),
        ),
        check_vma=False,
    )
```

```python
import functools

import jax
import jax.numpy as jnp
from jax import lax
from jax.experimental import pallas as pl
from jax.experimental.pallas import tpu as pltpu
from jax.sharding import PartitionSpec as P

MESH = pl.DeviceIdType.MESH
BF = jnp.bfloat16
F32 = jnp.float32
GROUPS, SLOTS, OWN, DM, HID = 8, 512, 32, 4096, 448
DS = DM // GROUPS
ROWS = GROUPS * SLOTS
H2, H3 = 2 * HID, 3 * HID
BR = 256
T = 16
TB = BR // T
PLANS = ((8, ((0, 3, 768), (3, 8, 768))), (10, ((0, 4, 1024), (4, 10, 1024))))
VLIM = 60 * 1024 * 1024


def rcopy(src, dst, ssem, rsem, dev):
    return pltpu.make_async_remote_copy(
        src_ref=src, dst_ref=dst, send_sem=ssem, recv_sem=rsem,
        device_id=dev, device_id_type=MESH,
    )


def spot(g, s):
    return (s + 3 * g + 8 * (s // 16)) % 16


def origin(g, m, j):
    return 16 * m + (j + 32 - 3 * g - 8 * m) % 16


def plane(axis, pos, j):
    y, x = j // 4, j % 4
    return {"et": y * 4 + pos % 4} if axis == "x" else {"et": (pos % 4) * 4 + x}


def greet(near, others):
    bar = pltpu.get_barrier_semaphore()
    for dev in near:
        pl.semaphore_signal(bar, inc=1, device_id=dev, device_id_type=MESH)
    for dd, jj in others:
        pl.semaphore_signal(bar, inc=1, device_id={"dp": dd, "et": jj}, device_id_type=MESH)
    pl.semaphore_wait(bar, len(near) + len(others))


def deliver(me, src, dst, ssem, rsem, dd, jj):
    d, j = me
    here = jnp.logical_and(dd == d, jj == j)
    far = rcopy(src, dst, ssem, rsem, {"dp": dd, "et": jj})

    @pl.when(here)
    def _():
        pltpu.make_async_copy(src, dst, rsem).start()

    @pl.when(jnp.logical_not(here))
    def _():
        far.start()

    def finish():
        @pl.when(jnp.logical_not(here))
        def _():
            far.wait_send()

    return finish


def gather_kernel(cap, tab, rows_ref, oc_ref, rw_ref, xg, sg,
                  sc, rb0, rb1, stage, psend, precv, osem, rsend, rrecv):
    d, j = lax.axis_index("dp"), lax.axis_index("et")
    me = (d, j)
    y, x = j // 4, j % 4
    lo = cap // 2
    senders = [((d + 8 - k) % 8, origin((d + 8 - k) % 8, m, j) // 2) for k in range(8) for m in range(2)]
    greet([plane("x", x + 1, j), plane("x", x + 3, j), plane("y", y + 1, j), plane("y", y + 3, j)],
          senders)
    mm = j // 8
    rb = (rb0, rb1)
    done = []
    arrays = []
    for a, (src, out, first, second) in enumerate(
        ((rows_ref, xg, "x", "y"), (sc, sg, "y", "x"))
    ):
        if a == 1:
            sc[...] = (rw_ref[...] * oc_ref[...].astype(F32)).astype(BF)
        for k in range(8):
            dd = (d + k) % 8
            cols = pl.ds(pl.multiple_of(dd * DS, DS), DS)
            for hh in range(2):
                jj = spot(d, 2 * j + hh)
                done.append(deliver(me, src.at[pl.ds(T * hh, T), cols], rb[a].at[2 * d + mm],
                                    psend.at[a, k, hh], precv.at[a, k, mm], dd, jj))
        p, q = (x, y) if first == "x" else (y, x)

        def blk(pp, qq, half=None, out=out, first=first):
            yy, xx = (qq % 4, pp % 4) if first == "x" else (pp % 4, qq % 4)
            g = slice(None) if half is None else (pl.ds(0, lo) if half == 0 else pl.ds(lo, cap - lo))
            return out.at[yy, xx, g]

        def send(i, ref, axis, pos, a=a, own=None):
            c = rcopy(ref if own is None else own, ref, rsend.at[a, i], rrecv.at[a, i], plane(axis, pos, j))
            c.start()
            return c

        arrays.append((p, q, first, second, blk, send))

    sent = [dict(), dict()]

    def second_sends(a, u, own=None):
        p, q, first, second, blk, send = arrays[a]
        base = 4 + 4 * (u % 4)
        sent[a][base] = send(base, blk(p + u, q), second, q + 1, own=own)
        sent[a][base + 1] = send(base + 1, blk(p + u, q), second, q + 3, own=own)

    def second_forward(a, u):
        p, q, first, second, blk, send = arrays[a]
        base = 4 + 4 * (u % 4)
        sent[a][base].wait_recv()
        sent[a][base + 2] = send(base + 2, blk(p + u, q + 3, 0), second, q + 1)
        sent[a][base + 1].wait_recv()
        sent[a][base + 3] = send(base + 3, blk(p + u, q + 1, 1), second, q + 3)

    keep = []
    for a in range(2):
        p, q, first, second, blk, send = arrays[a]
        for k in range(8):
            for m in range(2):
                g = (d + 8 - k) % 8
                pltpu.make_async_copy(rb[a].at[2 * g + m], rb[a].at[2 * g + m], precv.at[a, k, m]).wait()
        for i in range(cap):
            stage[a, i] = rb[a][tab[j, i]]
        sent[a][0] = send(0, blk(p, q), first, p + 1, own=stage.at[a])
        sent[a][1] = send(1, blk(p, q), first, p + 3, own=stage.at[a])
        second_sends(a, 0, own=stage.at[a])
        c = pltpu.make_async_copy(stage.at[a], blk(p, q), osem.at[a])
        c.start()
        keep.append(c)
    for a in range(2):
        p, q, first, second, blk, send = arrays[a]
        sent[a][0].wait_recv()
        sent[a][2] = send(2, blk(p + 3, q, 0), first, p + 1)
        second_sends(a, 3)
        sent[a][1].wait_recv()
        sent[a][3] = send(3, blk(p + 1, q, 1), first, p + 3)
        second_sends(a, 1)
    for a in range(2):
        second_forward(a, 0)
    for a in range(2):
        sent[a][2].wait_recv()
        sent[a][3].wait_recv()
        second_sends(a, 2)
    for u in (3, 1, 2):
        for a in range(2):
            second_forward(a, u)
    for a in range(2):
        keep[a].wait()
        for u in range(4):
            sent[a][6 + 4 * u].wait_recv()
            sent[a][7 + 4 * u].wait_recv()
        for c in sent[a].values():
            c.wait_send()
    for f in done:
        f()


def gather_rows(cap, cid, tab, rows, oc, rw):
    shape = jax.ShapeDtypeStruct((4, 4, cap, T, DS), BF)
    vm = pl.BlockSpec(memory_space=pltpu.VMEM)
    return pl.pallas_call(
        functools.partial(gather_kernel, cap),
        out_shape=(shape, shape),
        in_specs=[pl.BlockSpec(memory_space=pltpu.SMEM), vm, vm, vm],
        out_specs=(pl.BlockSpec(memory_space=pl.ANY),) * 2,
        scratch_shapes=[
            pltpu.VMEM((OWN, DM), BF),
            pltpu.VMEM((16, T, DS), BF),
            pltpu.VMEM((16, T, DS), BF),
            pltpu.VMEM((2, cap, T, DS), BF),
            pltpu.SemaphoreType.DMA((2, 8, 2)),
            pltpu.SemaphoreType.DMA((2, 8, 2)),
            pltpu.SemaphoreType.DMA((2,)),
            pltpu.SemaphoreType.DMA((2, 20)),
            pltpu.SemaphoreType.DMA((2, 20)),
        ],
        compiler_params=pltpu.CompilerParams(
            collective_id=cid, has_side_effects=True, vmem_limit_bytes=VLIM),
        name="gather_rows_%d" % cap,
    )(tab, rows, oc, rw)


def segments(cnt):
    segs, t = [], 0
    ends = []
    for e in range(2):
        row = []
        for g in range(GROUPS):
            c = cnt[g, e]
            first = 0 if e == 0 else (cnt[g, 0] + 127) // 128 * 8
            n = (c + T - 1) // T
            row.append((c, first, n, t))
            t = t + n
        ends.append(t)
        t = (t + TB - 1) // TB * TB
        ends.append(t)
        segs.append(row)
    return segs, ends


def tile(i):
    return pl.ds(pl.multiple_of(i * T, T), T)


def rows_of(b):
    return pl.ds(pl.multiple_of(b * BR, BR), BR)


def weight_copies(wg, wu, wd, wb, wsem):
    d = lax.axis_index("dp")
    cols = pl.ds(pl.multiple_of(d * DS, DS), DS)
    return [pltpu.make_async_copy(w.at[:, :, cols], wb.at[:, pl.ds(i * HID, HID), :], wsem.at[i])
            for i, w in enumerate((wg, wu, wd))]


TRANS_R = (((1,), (1,)), ((), ()))
TRANS_L = (((0,), (0,)), ((), ()))


def first_kernel(cap, cnt, tab, xg, sg, wg, wu, wd, part, xc_o, sc_o,
                 xv, sv, xc, sc, wb, pv, rsem, wsem, osem):
    segs, ends = segments(cnt)
    loads = [pltpu.make_async_copy(xg, xv, rsem.at[0]), pltpu.make_async_copy(sg, sv, rsem.at[1])]
    wcp = weight_copies(wg, wu, wd, wb, wsem)
    for c in loads + wcp:
        c.start()
    for c in loads:
        c.wait()
    zeros = jnp.zeros((T, DS), BF)
    iota = lax.broadcasted_iota(jnp.int32, (T, DS), 0)

    def source(g, s):
        jj = spot(g, s)
        return tile(jj * cap + tab[16 + jj, 2 * g + s // 16])

    for e in range(2):
        for g in range(GROUPS):
            c, first, n, t0 = segs[e][g]

            def move(k, _, g=g, first=first, t0=t0):
                src = source(g, first + k)
                xc[tile(t0 + k), :] = xv[src, :]
                sc[tile(t0 + k), :] = sv[src, :]
                return 0

            lax.fori_loop(0, n - 1, move, 0)
            keep = iota < c - T * (n - 1)
            src = source(g, first + n - 1)
            xt = xv[src, :].astype(F32)
            st = sv[src, :].astype(F32)
            xc[tile(t0 + n - 1), :] = jnp.where(keep, xt, 0.0).astype(BF)
            sc[tile(t0 + n - 1), :] = jnp.where(keep, st, 0.0).astype(BF)

        def blank(t, _):
            xc[tile(t), :] = zeros
            sc[tile(t), :] = zeros
            return 0

        lax.fori_loop(ends[2 * e], ends[2 * e + 1], blank, 0)
    for c in wcp:
        c.wait()
    nb0, nb = ends[1] // TB, ends[3] // TB

    def out_copies(b):
        rows = rows_of(b)
        return (pltpu.make_async_copy(pv.at[rows], part.at[rows], osem.at[0]),
                pltpu.make_async_copy(xc.at[rows], xc_o.at[rows], osem.at[1]),
                pltpu.make_async_copy(sc.at[rows], sc_o.at[rows], osem.at[2]))

    def block(b, _):
        e = (b >= nb0).astype(jnp.int32)
        rows = rows_of(b)
        pv[rows, 0:H2] = lax.dot_general(
            xc[rows, :], wb[e, 0:H2, :], TRANS_R, preferred_element_type=F32).astype(BF)
        pv[rows, H2:H3] = lax.dot_general(
            sc[rows, :], wb[e, H2:H3, :], TRANS_R, preferred_element_type=F32).astype(BF)
        for c in out_copies(b):
            c.start()
        return 0

    lax.fori_loop(0, nb, block, 0)

    def drain(b, _):
        for c in out_copies(b):
            c.wait()
        return 0

    lax.fori_loop(0, nb, drain, 0)


def first_matmuls(cap, rmax, counts, tab, xg, sg, wg, wu, wd):
    any_ = pl.BlockSpec(memory_space=pl.ANY)
    sm = pl.BlockSpec(memory_space=pltpu.SMEM)
    n = 16 * cap * T
    return pl.pallas_call(
        functools.partial(first_kernel, cap),
        out_shape=(jax.ShapeDtypeStruct((rmax, H3), BF),
                   jax.ShapeDtypeStruct((rmax, DS), BF),
                   jax.ShapeDtypeStruct((rmax, DS), BF)),
        in_specs=[sm, sm] + [any_] * 5,
        out_specs=(any_,) * 3,
        scratch_shapes=[
            pltpu.VMEM((n, DS), BF), pltpu.VMEM((n, DS), BF),
            pltpu.VMEM((rmax, DS), BF), pltpu.VMEM((rmax, DS), BF),
            pltpu.VMEM((2, H3, DS), BF),
            pltpu.VMEM((rmax, H3), BF),
            pltpu.SemaphoreType.DMA((2,)), pltpu.SemaphoreType.DMA((3,)),
            pltpu.SemaphoreType.DMA((3,)),
        ],
        compiler_params=pltpu.CompilerParams(vmem_limit_bytes=VLIM),
        name="first_matmuls_%d" % cap,
    )(counts, tab, xg.reshape(n, DS), sg.reshape(n, DS), wg, wu, wd)


def exchange_kernel(r, p, h, own, prt, q, l1, r1, s1, s2, l2, r2, tot, res,
                    osem, psend, precv, bsend, brecv, gsend, grecv, lsem):
    d = lax.axis_index("dp")
    z, c = d // 2, d % 2
    r8, r16 = r // 8, r // 16
    up, down = {"dp": (z + 1) % 4 * 2 + c}, {"dp": (z + 3) % 4 * 2 + c}
    mate = {"dp": z * 2 + 1 - c}
    bar = pltpu.get_barrier_semaphore()
    for dev in (up, down, mate):
        pl.semaphore_signal(bar, inc=1, device_id=dev, device_id_type=MESH)
    pl.semaphore_wait(bar, 3)

    def rows(zz, cc):
        return pl.ds(pl.multiple_of((zz % 4 * 2 + cc) * r8, r16), r8)

    def half(zz, cc, i):
        return pl.ds(pl.multiple_of((zz % 4 * 2 + cc) * r8 + i * r16, r16), r16)

    first, second = pl.ds(0, r16), pl.ds(r16, r16)
    pair, mine = {}, {}
    for i in (2, 1, 3, 0):
        pair[i] = rcopy(p.at[rows(z + i, 1 - c)], prt.at[i], psend.at[i], precv.at[i], mate)
        pair[i].start()
        mine[i] = pltpu.make_async_copy(p.at[rows(z + i, c)], own.at[i], osem.at[i])
        mine[i].start()

    def bsum(i):
        mine[i].wait()
        pair[i].wait_recv()

        def one(k, _):
            q[i, tile(k), :] = (own[i, tile(k), :].astype(F32) + prt[i, tile(k), :].astype(F32)).astype(BF)
            return 0

        lax.fori_loop(0, r8 // T, one, 0)

    def add_rows(dst, src, i, off):
        def one(k, _):
            dst[tile(k), :] = (src[tile(k), :].astype(F32) + q[i, tile(off + k), :].astype(F32)).astype(BF)
            return 0

        lax.fori_loop(0, r16 // T, one, 0)

    cps = []

    def push(i, src, dst, dev):
        cp = rcopy(src, dst, bsend.at[i], brecv.at[i], dev)
        cp.start()
        cps.append(cp)
        return cp

    bsum(2)
    a_l = push(0, q.at[2, first], l1, up)
    a_r = push(1, q.at[2, second], r1, down)
    bsum(1)
    b_l2 = push(2, q.at[1, second], l2.at[second], up)
    bsum(3)
    b_r1 = push(3, q.at[3, first], r2.at[first], down)
    a_l.wait_recv()
    add_rows(s1, l1, 1, 0)
    b_l1 = push(4, s1, l2.at[first], up)
    a_r.wait_recv()
    add_rows(s2, r1, 3, r16 // T)
    b_r2 = push(5, s2, r2.at[second], down)
    mine[0].wait()
    pair[0].wait_recv()
    for cp in (b_l2, b_r1, b_l1, b_r2):
        cp.wait_recv()

    def final(k, _):
        t = tile(k)
        tot[...] = (own[0, t, :].astype(F32) + prt[0, t, :].astype(F32)
                    + l2[t, :].astype(F32) + r2[t, :].astype(F32))
        gate, lin, grad = tot[:, 0:HID], tot[:, HID:H2], tot[:, H2:H3]
        s = 1.0 / (1.0 + jnp.exp(-gate))
        act = gate * s
        res[t, 0:HID] = (grad * lin * s * (1.0 + gate * (1.0 - s))).astype(BF)
        res[t, HID:H2] = (grad * act).astype(BF)
        res[t, H2:H3] = (act * lin).astype(BF)
        return 0

    lax.fori_loop(0, r8 // T, final, 0)
    keep = pltpu.make_async_copy(res, h.at[rows(z, c)], lsem)
    keep.start()
    gps = {}

    def spread(i, src, dst, dev):
        cp = rcopy(src, dst, gsend.at[i], grecv.at[i], dev)
        cp.start()
        gps[i] = cp

    spread(0, res, h.at[rows(z, c)], up)
    spread(1, res, h.at[rows(z, c)], down)
    spread(2, res, h.at[rows(z, c)], mate)
    gps[0].wait_recv()
    spread(3, h.at[half(z + 3, c, 0)], h.at[half(z + 3, c, 0)], up)
    spread(4, h.at[rows(z + 3, c)], h.at[rows(z + 3, c)], mate)
    gps[1].wait_recv()
    spread(5, h.at[half(z + 1, c, 1)], h.at[half(z + 1, c, 1)], down)
    spread(6, h.at[rows(z + 1, c)], h.at[rows(z + 1, c)], mate)
    gps[3].wait_recv()
    spread(7, h.at[half(z + 2, c, 0)], h.at[half(z + 2, c, 0)], mate)
    gps[5].wait_recv()
    spread(8, h.at[half(z + 2, c, 1)], h.at[half(z + 2, c, 1)], mate)
    for i in (2, 4, 6, 7, 8):
        gps[i].wait_recv()
    keep.wait()
    for cp in list(pair.values()) + cps + list(gps.values()):
        cp.wait_send()


def exchange(r, rmax, cid, part):
    r8, r16 = r // 8, r // 16
    any_ = pl.BlockSpec(memory_space=pl.ANY)
    v = lambda *s: pltpu.VMEM(s + (H3,), BF)
    dma = lambda n: pltpu.SemaphoreType.DMA((n,))
    return pl.pallas_call(
        functools.partial(exchange_kernel, r),
        out_shape=jax.ShapeDtypeStruct((rmax, H3), BF),
        in_specs=[any_],
        out_specs=any_,
        scratch_shapes=[
            v(4, r8), v(4, r8), v(4, r8),
            v(r16), v(r16), v(r16), v(r16),
            v(r8), v(r8), pltpu.VMEM((T, H3), F32), v(r8),
            dma(4), dma(4), dma(4), dma(6), dma(6), dma(9), dma(9), pltpu.SemaphoreType.DMA,
        ],
        compiler_params=pltpu.CompilerParams(
            collective_id=cid, has_side_effects=True, vmem_limit_bytes=VLIM),
        name="exchange_%d_%d" % (cid, r),
    )(part)


def second_kernel(cap, cnt, tab, h, xc_i, sc_i, wg, wu, wd, o, gr, dg, du, dd,
                  hv, xc, sc, wb, ov, gv, au, ad, bsem, wsem):
    segs, ends = segments(cnt)
    nb0, nb = ends[1] // TB, ends[3] // TB
    wcp = weight_copies(wg, wu, wd, wb, wsem)

    def in_copies(b):
        rows = rows_of(b)
        return (pltpu.make_async_copy(h.at[rows], hv.at[rows], bsem.at[0, b]),
                pltpu.make_async_copy(xc_i.at[rows], xc.at[rows], bsem.at[1, b]),
                pltpu.make_async_copy(sc_i.at[rows], sc.at[rows], bsem.at[2, b]))

    for c in wcp:
        c.start()

    def begin(b, _):
        for c in in_copies(b):
            c.start()
        return 0

    lax.fori_loop(0, nb, begin, 0)
    au[...] = jnp.zeros_like(au)
    ad[...] = jnp.zeros_like(ad)
    for c in wcp:
        c.wait()

    def block(b, _):
        e = (b >= nb0).astype(jnp.int32)
        rows = rows_of(b)
        for c in in_copies(b):
            c.wait()
        ov[rows, :] = jnp.dot(hv[rows, H2:H3], wb[e, H2:H3, :], preferred_element_type=F32).astype(BF)
        gv[rows, :] = jnp.dot(hv[rows, 0:H2], wb[e, 0:H2, :], preferred_element_type=F32).astype(BF)
        au[e] += lax.dot_general(hv[rows, 0:H2], xc[rows, :], TRANS_L, preferred_element_type=F32)
        ad[e] += lax.dot_general(hv[rows, H2:H3], sc[rows, :], TRANS_L, preferred_element_type=F32)
        return 0

    lax.fori_loop(0, nb, block, 0)
    dg[...] = au[:, 0:HID, :].astype(BF)
    du[...] = au[:, HID:H2, :].astype(BF)
    dd[...] = ad[...].astype(BF)

    for e in range(2):
        for g in range(GROUPS):
            c, first, n, t0 = segs[e][g]

            def move(k, _, g=g, first=first, t0=t0):
                s = first + k
                jj = spot(g, s)
                dst = tile(jj * cap + tab[16 + jj, 2 * g + s // 16])
                o[dst, :] = ov[tile(t0 + k), :]
                gr[dst, :] = gv[tile(t0 + k), :]
                return 0

            lax.fori_loop(0, n, move, 0)


def second_matmuls(cap, rmax, counts, tab, h, xc, sc, wg, wu, wd):
    any_ = pl.BlockSpec(memory_space=pl.ANY)
    sm = pl.BlockSpec(memory_space=pltpu.SMEM)
    vm = pl.BlockSpec(memory_space=pltpu.VMEM)
    s = jax.ShapeDtypeStruct
    n = 16 * cap * T
    return pl.pallas_call(
        functools.partial(second_kernel, cap),
        out_shape=(s((n, DS), BF), s((n, DS), BF)) + (s((2, HID, DS), BF),) * 3,
        in_specs=[sm, sm] + [any_] * 6,
        out_specs=(vm,) * 5,
        scratch_shapes=[
            pltpu.VMEM((rmax, H3), BF),
            pltpu.VMEM((rmax, DS), BF), pltpu.VMEM((rmax, DS), BF),
            pltpu.VMEM((2, H3, DS), BF),
            pltpu.VMEM((rmax, DS), BF), pltpu.VMEM((rmax, DS), BF),
            pltpu.VMEM((2, H2, DS), F32), pltpu.VMEM((2, HID, DS), F32),
            pltpu.SemaphoreType.DMA((3, rmax // BR)), pltpu.SemaphoreType.DMA((3,)),
        ],
        compiler_params=pltpu.CompilerParams(vmem_limit_bytes=VLIM),
        name="second_matmuls_%d" % cap,
    )(counts, tab, h, xc, sc, wg, wu, wd)


def reduce_kernel(cap, tab, o_ref, g_ref, rw_ref, oc_ref, out_o, out_w, out_g,
                  l1, r1, s1, s2, l2, r2, acc, bl1, br1, bs1, bs2, bl2, br2, fin, ex, rec,
                  asend, arecv, bsend, brecv, psend, precv):
    d, j = lax.axis_index("dp"), lax.axis_index("et")
    me = (d, j)
    y, x = j // 4, j % 4
    owners = [((d + k) % 8, spot(d, 2 * j + hh)) for k in range(8) for hh in range(2)]
    greet([plane("x", x + 1, j), plane("x", x + 3, j), plane("y", y + 1, j), plane("y", y + 3, j)],
          owners)
    half = cap // 2
    lo, hi = pl.ds(0, half), pl.ds(half, cap - half)
    order = (2, 1, 3, 0)
    info = []
    cps = []
    for a, (src, first) in enumerate(((o_ref, "y"), (g_ref, "x"))):
        second = "x" if first == "y" else "y"
        p, q = (y, x) if first == "y" else (x, y)

        def blk(pp, qq, g, src=src, first=first):
            yy, xx = (pp % 4, qq % 4) if first == "y" else (qq % 4, pp % 4)
            return src.at[yy, xx, g]

        info.append((p, q, first, second, blk))

    def push(sems, key, src, dst, axis, pos):
        send, recv = sems
        cp = rcopy(src, dst, send.at[key], recv.at[key], plane(axis, pos, j))
        cp.start()
        cps.append(cp)
        return cp

    def add2(dst, b, c):
        for g in range(half):
            dst[g] = (b[g].astype(F32) + c[g].astype(F32)).astype(BF)

    A, B = (asend, arecv), (bsend, brecv)
    av = [dict(), dict()]
    for u in order:
        for a in range(2):
            p, q, first, second, blk = info[a]
            av[a][u, 0] = push(A, (a, u, 0), blk(p + 2, q + u, lo), l1.at[a, u], first, p + 1)
            av[a][u, 1] = push(A, (a, u, 1), blk(p + 2, q + u, hi), r1.at[a, u], first, p + 3)
            av[a][u, 2] = push(A, (a, u, 2), blk(p + 1, q + u, hi), l2.at[a, u, hi], first, p + 1)
            av[a][u, 3] = push(A, (a, u, 3), blk(p + 3, q + u, lo), r2.at[a, u, lo], first, p + 3)
    for u in order:
        for a in range(2):
            p, q, first, second, blk = info[a]
            av[a][u, 0].wait_recv()
            add2(s1.at[a, u], l1.at[a, u], blk(p + 1, q + u, lo))
            av[a][u, 4] = push(A, (a, u, 4), s1.at[a, u], l2.at[a, u, lo], first, p + 1)
            av[a][u, 1].wait_recv()
            add2(s2.at[a, u], r1.at[a, u], blk(p + 3, q + u, hi))
            av[a][u, 5] = push(A, (a, u, 5), s2.at[a, u], r2.at[a, u, hi], first, p + 3)
    bv = [dict(), dict()]
    for u in order:
        for a in range(2):
            p, q, first, second, blk = info[a]
            for i in (2, 3, 4, 5):
                av[a][u, i].wait_recv()
            mine = blk(p, q + u, pl.ds(0, cap))
            for g in range(cap):
                acc[a, u, g] = (mine[g].astype(F32) + l2[a, u, g].astype(F32)
                                + r2[a, u, g].astype(F32)).astype(BF)
            if u == 2:
                bv[a][0] = push(B, (a, 0), acc.at[a, 2, lo], bl1.at[a], second, q + 1)
                bv[a][1] = push(B, (a, 1), acc.at[a, 2, hi], br1.at[a], second, q + 3)
            elif u == 1:
                bv[a][2] = push(B, (a, 2), acc.at[a, 1, hi], bl2.at[a, hi], second, q + 1)
            elif u == 3:
                bv[a][3] = push(B, (a, 3), acc.at[a, 3, lo], br2.at[a, lo], second, q + 3)
    for a in range(2):
        p, q, first, second, blk = info[a]
        bv[a][0].wait_recv()
        add2(bs1.at[a], bl1.at[a], acc.at[a, 1, lo])
        bv[a][4] = push(B, (a, 4), bs1.at[a], bl2.at[a, lo], second, q + 1)
        bv[a][1].wait_recv()
        add2(bs2.at[a], br1.at[a], acc.at[a, 3, hi])
        bv[a][5] = push(B, (a, 5), bs2.at[a], br2.at[a, hi], second, q + 3)
    done = []
    for a in range(2):
        for i in (2, 3, 4, 5):
            bv[a][i].wait_recv()
        for g in range(cap):
            fin[a, g] = (acc[a, 0, g].astype(F32) + bl2[a, g].astype(F32)
                         + br2[a, g].astype(F32)).astype(BF)
        for k in range(8):
            g = (d + k) % 8
            for m in range(2):
                s = origin(g, m, j)
                at = tab[16 + j, 2 * g + m]
                got = fin[a, jnp.maximum(at, 0)].astype(F32)
                ex[a, k, m] = jnp.where(at >= 0, got, 0.0).astype(BF)
                done.append(deliver(me, ex.at[a, k, m], rec.at[a, d, s % 2],
                                    psend.at[a, k, m], precv.at[a, k, s % 2], g, s // 2))
    for a in range(2):
        for k in range(8):
            for hh in range(2):
                spot_ref = rec.at[a, (d + 8 - k) % 8, hh]
                pltpu.make_async_copy(spot_ref, spot_ref, precv.at[a, k, hh]).wait()
    rw = rw_ref[...]
    total = jnp.zeros((OWN, 1), F32)
    for k in range(8):
        cols = slice(k * DS, (k + 1) * DS)
        comb = rec[0, k].astype(F32).reshape(OWN, DS)
        out_o[:, cols] = (rw * comb).astype(BF)
        total = total + jnp.sum(oc_ref[:, cols].astype(F32) * comb, axis=1, keepdims=True)
        out_g[:, cols] = rec[1, k].reshape(OWN, DS)
    out_w[...] = total
    for cp in cps:
        cp.wait_send()
    for f in done:
        f()


def reduce_rows(cap, cid, tab, o, g, rw, oc):
    vm = pl.BlockSpec(memory_space=pltpu.VMEM)
    s = jax.ShapeDtypeStruct
    v = lambda *sh: pltpu.VMEM(sh + (T, DS), BF)
    dma = lambda *n: pltpu.SemaphoreType.DMA(n)
    h = cap // 2
    return pl.pallas_call(
        functools.partial(reduce_kernel, cap),
        out_shape=(s((OWN, DM), BF), s((OWN, 1), F32), s((OWN, DM), BF)),
        in_specs=[pl.BlockSpec(memory_space=pltpu.SMEM)] + [vm] * 4,
        out_specs=(vm,) * 3,
        scratch_shapes=[
            v(2, 4, h), v(2, 4, h), v(2, 4, h), v(2, 4, h), v(2, 4, cap), v(2, 4, cap), v(2, 4, cap),
            v(2, h), v(2, h), v(2, h), v(2, h), v(2, cap), v(2, cap), v(2, cap),
            v(2, 8, 2), v(2, 8, 2),
            dma(2, 4, 6), dma(2, 4, 6), dma(2, 6), dma(2, 6), dma(2, 8, 2), dma(2, 8, 2),
        ],
        compiler_params=pltpu.CompilerParams(
            collective_id=cid, has_side_effects=True, vmem_limit_bytes=VLIM),
        name="reduce_rows_%d" % cap,
    )(tab, o.reshape(4, 4, cap, T, DS), g.reshape(4, 4, cap, T, DS), rw, oc)


def plan_kernel(plans, cnt, out):
    i32 = lambda v: v.astype(jnp.int32)
    f = lambda v: v.astype(F32)
    j = lax.broadcasted_iota(jnp.int32, (16, 16), 0)
    q = lax.broadcasted_iota(jnp.int32, (16, 16), 1)
    g, m = q // 2, q % 2
    s = origin(g, m, j)
    c0 = jnp.zeros((16, 16), jnp.int32)
    c1 = jnp.zeros((16, 16), jnp.int32)
    for k in range(GROUPS):
        c0 = jnp.where(g == k, cnt[k, 0], c0)
        c1 = jnp.where(g == k, cnt[k, 1], c1)
    s1 = (c0 + 127) // 128 * 8
    left0 = jnp.clip(c0 - T * s, 0, T)
    left1 = jnp.where(s >= s1, jnp.clip(c1 - T * (s - s1), 0, T), 0)
    live = left0 + left1 > 0
    one = f(i32(live))
    mm = lambda a, b, dims: lax.dot_general(a, b, (dims, ((), ())), preferred_element_type=F32,
                                            precision=lax.Precision.HIGHEST)
    rank = mm(one, f(i32(j < q)), ((1,), (0,)))
    place = jnp.where(live, i32(rank), -1)
    orders = jnp.zeros((16, 16), jnp.int32)
    rows0 = jnp.zeros((16, 16), jnp.int32)
    rows1 = jnp.zeros((16, 16), jnp.int32)
    for k in range(16):
        hit = place == k
        pick = lambda v: jnp.sum(f(jnp.where(hit, v, 0)), axis=1, keepdims=True)
        orders = jnp.where(q == k, i32(pick(q)), orders)
        rows0 = jnp.where(q == k, i32(pick(left0)), rows0)
        rows1 = jnp.where(q == k, i32(pick(left1)), rows1)
    out[...] = jnp.zeros_like(out)
    out[0:16, 0:16] = orders
    out[16:32, 0:16] = place
    nrow = mm(jnp.ones((8, 16), F32), one, ((1,), (1,)))[0:1, :]
    ok = []
    base = 32
    for cap, chunks in plans:
        fits = jnp.max(nrow) <= cap
        for lo, hi, r in chunks:
            nt = r // T
            n = jnp.clip(nrow - lo, 0.0, float(hi - lo))
            n8 = jnp.broadcast_to(n, (8, 16))
            off = mm(n8, f(i32(j < q)), ((1,), (0,)))[0:1, :]
            t = lax.broadcasted_iota(jnp.int32, (nt, 16), 0)
            qq = lax.broadcasted_iota(jnp.int32, (nt, 16), 1)
            offb, nb = jnp.broadcast_to(off, (nt, 16)), jnp.broadcast_to(n, (nt, 16))
            hot = f(i32((f(t) >= offb) & (f(t) < offb + nb)))
            at = jnp.sum(hot * (f(t) - offb), axis=1, keepdims=True)
            dev = jnp.sum(hot * f(qq), axis=1, keepdims=True)
            used = jnp.sum(hot, axis=1, keepdims=True)
            col = f(i32(f(qq) == at + float(lo)))
            sel = lambda v: jnp.sum(col * mm(hot, f(v), ((1,), (0,))), axis=1, keepdims=True) * used
            out[base:base + nt, 0:1] = i32(dev * float(hi - lo) + at)
            out[base:base + nt, 1:2] = i32(sel(rows0))
            out[base:base + nt, 2:3] = i32(sel(rows1))
            ncol = jnp.clip(jnp.sum(one, axis=1, keepdims=True) - lo, 0.0, float(hi - lo))
            ocol = mm(f(i32(q < j)), jnp.broadcast_to(ncol, (16, 8)), ((1,), (0,)))[:, 0:1]
            back = jnp.clip(i32(ocol) + q - lo, 0, nt - 1)
            out[base + nt:base + nt + 16, 0:16] = back + jnp.where(rows1 > 0, nt, 0)
            base += nt + 16
            fits = jnp.logical_and(fits, jnp.sum(n) <= nt)
        ok.append(fits)
    level = jnp.int32(len(plans))
    for i in range(len(plans) - 1, -1, -1):
        level = jnp.where(ok[i], i, level)
    lane = lax.broadcasted_iota(jnp.int32, (8, 16), 1)
    out[base:base + 8, 0:16] = jnp.where(lane == 0, level, 0)


def table_base(plans, index):
    base = 32
    for cap, chunks in plans[:index]:
        for lo, hi, r in chunks:
            base += r // T + 16
    return base


def plan_table(plans, counts):
    rows = table_base(plans, len(plans)) + 8
    return pl.pallas_call(
        functools.partial(plan_kernel, plans),
        out_shape=jax.ShapeDtypeStruct((rows, 16), jnp.int32),
        in_specs=[pl.BlockSpec(memory_space=pltpu.SMEM)],
        out_specs=pl.BlockSpec(memory_space=pltpu.VMEM),
        name="tile_plan",
    )(counts)


def layer_kernel(cap, chunks, base, tab, rows_ref, oc_ref, rw_ref, wg, wu, wd,
                 out_o, out_w, out_g, dg, du, dd_o, sc, rb0, rb1, stage, wcat, xcat, scat, hall,
                 ov, gv, fin, ex, rec, *rest):
    d, j = lax.axis_index("dp"), lax.axis_index("et")
    me = (d, j)
    y, x = j // 4, j % 4
    z, c = d // 2, d % 2
    nch = len(chunks)
    names = ("xg", "sg", "part", "prt", "q", "zl1", "zr1", "zs1", "zs2", "zl2", "zr2", "tot",
             "ob", "gb", "l1", "r1", "s1", "s2", "l2", "r2", "acc", "bl1", "br1", "bs1", "bs2", "bl2", "br2")
    buf = [dict(zip(names, rest[i * len(names):(i + 1) * len(names)])) for i in range(nch)]
    (psend, precv, wsem, rsend, rrecv, zps, zpr, zbs, zbr, zgs, zgr,
     asend, arecv, bsend, brecv, qsend, qrecv) = rest[nch * len(names):]
    up, down = {"dp": (z + 1) % 4 * 2 + c}, {"dp": (z + 3) % 4 * 2 + c}
    mate = {"dp": z * 2 + 1 - c}
    owners = [((d + k) % 8, spot(d, 2 * j + hh)) for k in range(8) for hh in range(2)]
    senders = [((d + 8 - k) % 8, origin((d + 8 - k) % 8, m, j) // 2) for k in range(8) for m in range(2)]
    greet([plane("x", x + 1, j), plane("x", x + 3, j), plane("y", y + 1, j), plane("y", y + 3, j),
           up, down, mate], owners + senders)
    finish = []
    rb = (rb0, rb1)
    offs = []
    b = base
    for lo, hi, r in chunks:
        offs.append(b)
        b += r // T + 16
    first_row = [sum(r for _, _, r in chunks[:i]) for i in range(nch)]

    def remote(src, dst, ssem, rsem, dev):
        cp = rcopy(src, dst, ssem, rsem, dev)
        cp.start()
        finish.append(cp.wait_send)
        return cp

    mm = j // 8
    cols = pl.ds(pl.multiple_of(d * DS, DS), DS)
    wcp = []
    for a, src in enumerate((rows_ref, sc)):
        if a == 1:
            eye = lax.broadcasted_iota(jnp.int32, (OWN, OWN), 0) == lax.broadcasted_iota(jnp.int32, (OWN, OWN), 1)
            rw = jnp.sum(jnp.where(eye, jnp.broadcast_to(rw_ref[...], (OWN, OWN)), 0.0), axis=1, keepdims=True)
            for k in range(8):
                cs = slice(k * DS, (k + 1) * DS)
                sc[:, cs] = (rw * oc_ref[:, cs].astype(F32)).astype(BF)
        for k in range(8):
            dd = (d + k) % 8
            cs = pl.ds(pl.multiple_of(dd * DS, DS), DS)
            for hh in range(2):
                jj = spot(d, 2 * j + hh)
                finish.append(deliver(me, src.at[pl.ds(T * hh, T), cs], rb[a].at[2 * d + mm],
                                      psend.at[a, k, hh], precv.at[a, k, mm], dd, jj))
    for e in range(2):
        for i, w in enumerate((wg, wu, wd)):
            cp = pltpu.make_async_copy(w.at[e, :, cols],
                                       wcat.at[pl.ds(i * HID, HID), pl.ds(e * DS, DS)], wsem.at[e, i])
            cp.start()
            wcp.append(cp)

    def arrive(a):
        for k in range(8):
            for m in range(2):
                ref = rb[a].at[2 * ((d + 8 - k) % 8) + m]
                pltpu.make_async_copy(ref, ref, precv.at[a, k, m]).wait()
        for i in range(cap):
            stage[a, i] = rb[a][tab[j, i]]

    def gather(ch):
        lo, hi, r = chunks[ch]
        nt = hi - lo
        h0 = nt // 2
        ax = (("x", "y", x, y), ("y", "x", y, x))
        outs = (buf[ch]["xg"], buf[ch]["sg"])

        def blk(a, pp, qq, half=None):
            yy, xx = (qq % 4, pp % 4) if a == 0 else (pp % 4, qq % 4)
            off, n = (0, nt) if half is None else ((0, h0) if half == 0 else (h0, nt - h0))
            return outs[a].at[pl.ds((4 * yy + xx) * nt + off, n)]

        sent = [dict(), dict()]

        def send(a, i, ref, axis, pos, own=None):
            sent[a][i] = remote(ref if own is None else own, ref, rsend.at[ch, a, i], rrecv.at[ch, a, i],
                                plane(axis, pos, j))

        def seconds(a, u, own=None):
            first, second, p, q = ax[a]
            i = 4 + 4 * (u % 4)
            send(a, i, blk(a, p + u, q), second, q + 1, own)
            send(a, i + 1, blk(a, p + u, q), second, q + 3, own)

        def forward(a, u):
            first, second, p, q = ax[a]
            i = 4 + 4 * (u % 4)
            sent[a][i].wait_recv()
            send(a, i + 2, blk(a, p + u, q + 3, 0), second, q + 1)
            sent[a][i + 1].wait_recv()
            send(a, i + 3, blk(a, p + u, q + 1, 1), second, q + 3)

        for a in range(2):
            first, second, p, q = ax[a]
            if ch == 0:
                arrive(a)
            own = stage.at[a, pl.ds(lo, nt)]
            send(a, 0, blk(a, p, q), first, p + 1, own)
            send(a, 1, blk(a, p, q), first, p + 3, own)
            seconds(a, 0, own)
            outs[a][pl.ds(j * nt, nt)] = stage[a, lo:hi]
        yield
        for a in range(2):
            first, second, p, q = ax[a]
            sent[a][0].wait_recv()
            send(a, 2, blk(a, p + 3, q, 0), first, p + 1)
            seconds(a, 3)
            sent[a][1].wait_recv()
            send(a, 3, blk(a, p + 1, q, 1), first, p + 3)
            seconds(a, 1)
            yield
        for a in range(2):
            forward(a, 0)
            yield
        for a in range(2):
            sent[a][2].wait_recv()
            sent[a][3].wait_recv()
            seconds(a, 2)
        yield
        for u in (3, 1, 2):
            for a in range(2):
                forward(a, u)
            yield
        for a in range(2):
            for u in range(4):
                sent[a][6 + 4 * u].wait_recv()
                sent[a][7 + 4 * u].wait_recv()

    def first(ch):
        lo, hi, r = chunks[ch]
        xg, sg, part = buf[ch]["xg"], buf[ch]["sg"], buf[ch]["part"]
        iota = lax.broadcasted_iota(jnp.int32, (T, DS), 0)
        r0 = first_row[ch]

        def pack(t, _):
            src = tab[offs[ch] + t, 0]
            xt, st = xg[src].astype(F32), sg[src].astype(F32)
            dst = tile(r0 // T + t)
            for e in range(2):
                keep = iota < tab[offs[ch] + t, 1 + e]
                cs = slice(e * DS, (e + 1) * DS)
                xcat[dst, cs] = jnp.where(keep, xt, 0.0).astype(BF)
                scat[dst, cs] = jnp.where(keep, st, 0.0).astype(BF)
            return 0

        lax.fori_loop(0, r // T, pack, 0)
        if ch == 0:
            for cp in wcp:
                cp.wait()

        def mul(i, _):
            src = pl.ds(pl.multiple_of(r0 + i * BR, BR), BR)
            dst = rows_of(i)
            part[dst, 0:H2] = lax.dot_general(
                xcat[src, :], wcat[0:H2, :], TRANS_R, preferred_element_type=F32).astype(BF)
            part[dst, H2:H3] = lax.dot_general(
                scat[src, :], wcat[H2:H3, :], TRANS_R, preferred_element_type=F32).astype(BF)
            return 0

        lax.fori_loop(0, r // BR, mul, 0)

    def exchange_chunk(ch):
        lo, hi, r = chunks[ch]
        bf = buf[ch]
        part, prt, q, tot = bf["part"], bf["prt"], bf["q"], bf["tot"]
        r8, r16 = r // 8, r // 16
        r0 = first_row[ch]
        fst, snd = pl.ds(0, r16), pl.ds(r16, r16)

        def rows(zz, cc, off=0, n=None):
            return pl.ds(pl.multiple_of((zz % 4 * 2 + cc) * r8 + off, 16), r8 if n is None else n)

        def hrows(zz, cc, off=0, n=None):
            return hall.at[pl.ds(pl.multiple_of(r0 + (zz % 4 * 2 + cc) * r8 + off, 16), r8 if n is None else n)]

        pair = {}
        for i in (2, 1, 3, 0):
            pair[i] = remote(part.at[rows(z + i, 1 - c)], prt.at[i], zps.at[ch, i], zpr.at[ch, i], mate)
        yield

        def bsum(i):
            pair[i].wait_recv()
            start = (z + i) % 4 * 2 + c

            def one(k, _):
                src = pl.ds(pl.multiple_of(start * r8 + k * T, T), T)
                q[i, tile(k), :] = (part[src, :].astype(F32) + prt[i, tile(k), :].astype(F32)).astype(BF)
                return 0

            lax.fori_loop(0, r8 // T, one, 0)

        def add_rows(dst, src, i, off):
            def one(k, _):
                dst[tile(k), :] = (src[tile(k), :].astype(F32) + q[i, tile(off + k), :].astype(F32)).astype(BF)
                return 0

            lax.fori_loop(0, r16 // T, one, 0)

        def push(i, src, dst, dev):
            return remote(src, dst, zbs.at[ch, i], zbr.at[ch, i], dev)

        bsum(2)
        a_l = push(0, q.at[2, fst], bf["zl1"], up)
        a_r = push(1, q.at[2, snd], bf["zr1"], down)
        bsum(1)
        b_l2 = push(2, q.at[1, snd], bf["zl2"].at[snd], up)
        bsum(3)
        b_r1 = push(3, q.at[3, fst], bf["zr2"].at[fst], down)
        yield
        a_l.wait_recv()
        add_rows(bf["zs1"], bf["zl1"], 1, 0)
        b_l1 = push(4, bf["zs1"], bf["zl2"].at[fst], up)
        a_r.wait_recv()
        add_rows(bf["zs2"], bf["zr1"], 3, r16 // T)
        b_r2 = push(5, bf["zs2"], bf["zr2"].at[snd], down)
        yield
        pair[0].wait_recv()
        for cp in (b_l2, b_r1, b_l1, b_r2):
            cp.wait_recv()
        mine = (z * 2 + c) * r8

        def final(k, _):
            t = tile(k)
            src = pl.ds(pl.multiple_of(mine + k * T, T), T)
            dst = pl.ds(pl.multiple_of(r0 + mine + k * T, T), T)
            tot[...] = (part[src, :].astype(F32) + prt[0, t, :].astype(F32)
                        + bf["zl2"][t, :].astype(F32) + bf["zr2"][t, :].astype(F32))
            gate, lin, grad = tot[:, 0:HID], tot[:, HID:H2], tot[:, H2:H3]
            s = 1.0 / (1.0 + jnp.exp(-gate))
            act = gate * s
            hall[dst, 0:HID] = (grad * lin * s * (1.0 + gate * (1.0 - s))).astype(BF)
            hall[dst, HID:H2] = (grad * act).astype(BF)
            hall[dst, H2:H3] = (act * lin).astype(BF)
            return 0

        lax.fori_loop(0, r8 // T, final, 0)
        gps = {}

        def spread(i, ref, dev):
            gps[i] = remote(ref, ref, zgs.at[ch, i], zgr.at[ch, i], dev)

        spread(0, hrows(z, c), up)
        spread(1, hrows(z, c), down)
        spread(2, hrows(z, c), mate)
        yield
        gps[0].wait_recv()
        spread(3, hrows(z + 3, c, 0, r16), up)
        spread(4, hrows(z + 3, c), mate)
        gps[1].wait_recv()
        spread(5, hrows(z + 1, c, r16, r16), down)
        spread(6, hrows(z + 1, c), mate)
        yield
        gps[3].wait_recv()
        spread(7, hrows(z + 2, c, 0, r16), mate)
        gps[5].wait_recv()
        spread(8, hrows(z + 2, c, r16, r16), mate)
        yield
        for i in (2, 4, 6, 7, 8):
            gps[i].wait_recv()

    def second(ch):
        lo, hi, r = chunks[ch]
        nt = hi - lo
        r0 = first_row[ch]
        ob, gb = buf[ch]["ob"], buf[ch]["gb"]

        def mul(i, _):
            src = pl.ds(pl.multiple_of(r0 + i * BR, BR), BR)
            for e in range(2):
                dst = pl.ds(e * (r // T) + i * TB, TB)
                cs = slice(e * DS, (e + 1) * DS)
                to = jnp.dot(hall[src, H2:H3], wcat[H2:H3, cs], preferred_element_type=F32).astype(BF)
                tg = jnp.dot(hall[src, 0:H2], wcat[0:H2, cs], preferred_element_type=F32).astype(BF)
                ov[dst] = to.reshape(TB, T, DS)
                gv[dst] = tg.reshape(TB, T, DS)
            return 0

        lax.fori_loop(0, r // BR, mul, 0)

        def unpack(jj, _):
            for i in range(nt):
                src = tab[offs[ch] + r // T + jj, lo + i]
                ob[jj, i] = ov[src]
                gb[jj, i] = gv[src]
            return 0

        lax.fori_loop(0, 16, unpack, 0)

    def reduce_chunk(ch):
        lo_t, hi_t, r = chunks[ch]
        nt = hi_t - lo_t
        h0 = nt // 2
        bf = buf[ch]
        lo, hi = pl.ds(0, h0), pl.ds(h0, nt - h0)
        srcs = (bf["ob"], bf["gb"])
        ax = (("y", "x", y, x), ("x", "y", x, y))
        order = (2, 1, 3, 0)

        def blk(a, pp, qq, g):
            yy, xx = (pp % 4, qq % 4) if a == 0 else (qq % 4, pp % 4)
            return srcs[a].at[4 * yy + xx, g]

        def push(sems, key, src, dst, axis, pos):
            return remote(src, dst, sems[0].at[(ch,) + key], sems[1].at[(ch,) + key], plane(axis, pos, j))

        def add2(n, dst, b, cc):
            for g in range(n):
                dst[g] = (b[g].astype(F32) + cc[g].astype(F32)).astype(BF)

        A, B = (asend, arecv), (bsend, brecv)
        av, bv = [dict(), dict()], [dict(), dict()]
        l1, r1, s1, s2, l2, r2, acc = (bf[k] for k in ("l1", "r1", "s1", "s2", "l2", "r2", "acc"))
        bl1, br1, bs1, bs2, bl2, br2 = (bf[k] for k in ("bl1", "br1", "bs1", "bs2", "bl2", "br2"))
        for u in order:
            for a in range(2):
                fx, sx, p, q = ax[a]
                av[a][u, 0] = push(A, (a, u, 0), blk(a, p + 2, q + u, lo), l1.at[a, u], fx, p + 1)
                av[a][u, 1] = push(A, (a, u, 1), blk(a, p + 2, q + u, hi), r1.at[a, u], fx, p + 3)
                av[a][u, 2] = push(A, (a, u, 2), blk(a, p + 1, q + u, hi), l2.at[a, u, hi], fx, p + 1)
                av[a][u, 3] = push(A, (a, u, 3), blk(a, p + 3, q + u, lo), r2.at[a, u, lo], fx, p + 3)
        yield
        for u in order:
            for a in range(2):
                fx, sx, p, q = ax[a]
                av[a][u, 0].wait_recv()
                add2(h0, s1.at[a, u], l1.at[a, u], blk(a, p + 1, q + u, lo))
                av[a][u, 4] = push(A, (a, u, 4), s1.at[a, u], l2.at[a, u, lo], fx, p + 1)
                av[a][u, 1].wait_recv()
                add2(nt - h0, s2.at[a, u], r1.at[a, u], blk(a, p + 3, q + u, hi))
                av[a][u, 5] = push(A, (a, u, 5), s2.at[a, u], r2.at[a, u, hi], fx, p + 3)
            if u in (1, 0):
                yield
        for u in order:
            for a in range(2):
                fx, sx, p, q = ax[a]
                for i in (2, 3, 4, 5):
                    av[a][u, i].wait_recv()
                mine = blk(a, p, q + u, pl.ds(0, nt))
                for g in range(nt):
                    acc[a, u, g] = (mine[g].astype(F32) + l2[a, u, g].astype(F32)
                                    + r2[a, u, g].astype(F32)).astype(BF)
                if u == 2:
                    bv[a][0] = push(B, (a, 0), acc.at[a, 2, lo], bl1.at[a], sx, q + 1)
                    bv[a][1] = push(B, (a, 1), acc.at[a, 2, hi], br1.at[a], sx, q + 3)
                elif u == 1:
                    bv[a][2] = push(B, (a, 2), acc.at[a, 1, hi], bl2.at[a, hi], sx, q + 1)
                elif u == 3:
                    bv[a][3] = push(B, (a, 3), acc.at[a, 3, lo], br2.at[a, lo], sx, q + 3)
            if u in (1, 0):
                yield
        for a in range(2):
            fx, sx, p, q = ax[a]
            bv[a][0].wait_recv()
            add2(h0, bs1.at[a], bl1.at[a], acc.at[a, 1, lo])
            bv[a][4] = push(B, (a, 4), bs1.at[a], bl2.at[a, lo], sx, q + 1)
            bv[a][1].wait_recv()
            add2(nt - h0, bs2.at[a], br1.at[a], acc.at[a, 3, hi])
            bv[a][5] = push(B, (a, 5), bs2.at[a], br2.at[a, hi], sx, q + 3)
        yield
        for a in range(2):
            for i in (2, 3, 4, 5):
                bv[a][i].wait_recv()
            for g in range(nt):
                fin[a, lo_t + g] = (acc[a, 0, g].astype(F32) + bl2[a, g].astype(F32)
                                    + br2[a, g].astype(F32)).astype(BF)

    def weight_grads():
        n = 256

        def one(i, _):
            cs = pl.ds(pl.multiple_of(i * n, n), n)
            e, os = i // (DS // n), pl.ds(pl.multiple_of(i % (DS // n) * n, n), n)
            both = lax.dot_general(hall[:, 0:H2], xcat[:, cs], TRANS_L, preferred_element_type=F32)
            dg[e, :, os] = both[0:HID].astype(BF)
            du[e, :, os] = both[HID:H2].astype(BF)
            dd_o[e, :, os] = lax.dot_general(hall[:, H2:H3], scat[:, cs], TRANS_L,
                                             preferred_element_type=F32).astype(BF)
            return 0

        lax.fori_loop(0, 2 * DS // n, one, 0)

    def drain(gen):
        for _ in gen:
            pass

    def step(gen, n=1):
        for _ in range(n):
            if next(gen, 0) == 0:
                return False
        return True

    drain(gather(0))
    first(0)
    if nch == 2:
        za, gb_ = exchange_chunk(0), gather(1)
        step(za)
        more = True
        while step(za):
            more = more and step(gb_, 2)
        drain(gb_)
        first(1)
        zb = exchange_chunk(1)
        step(zb)
        second(0)
        ra = reduce_chunk(0)
        step(ra)
        while step(zb):
            step(ra)
        drain(ra)
        second(1)
        rl = reduce_chunk(1)
    else:
        drain(exchange_chunk(0))
        second(0)
        rl = reduce_chunk(0)
    step(rl)
    weight_grads()
    drain(rl)

    for a in range(2):
        for k in range(8):
            g = (d + k) % 8
            for m in range(2):
                s = origin(g, m, j)
                at = tab[16 + j, 2 * g + m]
                got = fin[a, jnp.maximum(at, 0)].astype(F32)
                ex[a, k, m] = jnp.where(at >= 0, got, 0.0).astype(BF)
                finish.append(deliver(me, ex.at[a, k, m], rec.at[a, d, s % 2],
                                      qsend.at[a, k, m], qrecv.at[a, k, s % 2], g, s // 2))
    total = jnp.zeros((OWN, 1), F32)
    for a in range(2):
        for k in range(8):
            for hh in range(2):
                ref = rec.at[a, (d + 8 - k) % 8, hh]
                pltpu.make_async_copy(ref, ref, qrecv.at[a, k, hh]).wait()
        for k in range(8):
            cs = slice(k * DS, (k + 1) * DS)
            if a == 0:
                comb = rec[0, k].astype(F32).reshape(OWN, DS)
                out_o[:, cs] = (rw * comb).astype(BF)
                total = total + jnp.sum(oc_ref[:, cs].astype(F32) * comb, axis=1, keepdims=True)
            else:
                out_g[:, cs] = rec[1, k].reshape(OWN, DS)
    out_w[...] = jnp.sum(jnp.where(eye, jnp.broadcast_to(total, (OWN, OWN)), 0.0), axis=0, keepdims=True)
    for f in finish:
        f()


def layer(plans, index, cid, tab, rows, oc, rw, wg, wu, wd):
    cap, chunks = plans[index]
    vm = pl.BlockSpec(memory_space=pltpu.VMEM)
    any_ = pl.BlockSpec(memory_space=pl.ANY)
    s = jax.ShapeDtypeStruct
    v = lambda *sh: pltpu.VMEM(sh, BF)
    tl = lambda *sh: pltpu.VMEM(sh + (T, DS), BF)
    dma = lambda *n: pltpu.SemaphoreType.DMA(n)
    total = sum(r for _, _, r in chunks)
    rbig = max(r for _, _, r in chunks)
    nch = len(chunks)
    scratch = [v(OWN, DM), tl(16), tl(16), tl(2, cap), v(H3, 2 * DS), v(total, 2 * DS), v(total, 2 * DS),
               v(total, H3), tl(2 * rbig // T), tl(2 * rbig // T), tl(2, cap), tl(2, 8, 2), tl(2, 8, 2)]
    for lo, hi, r in chunks:
        nt = hi - lo
        h0, h1 = nt // 2, nt - nt // 2
        r8, r16 = r // 8, r // 16
        scratch += [tl(16 * nt), tl(16 * nt), v(r, H3), v(4, r8, H3), v(4, r8, H3),
                    v(r16, H3), v(r16, H3), v(r16, H3), v(r16, H3), v(r8, H3), v(r8, H3),
                    pltpu.VMEM((T, H3), F32), tl(16, nt), tl(16, nt),
                    tl(2, 4, h0), tl(2, 4, h1), tl(2, 4, h0), tl(2, 4, h1),
                    tl(2, 4, nt), tl(2, 4, nt), tl(2, 4, nt),
                    tl(2, h0), tl(2, h1), tl(2, h0), tl(2, h1), tl(2, nt), tl(2, nt)]
    scratch += [dma(2, 8, 2), dma(2, 8, 2), dma(2, 3), dma(nch, 2, 20), dma(nch, 2, 20),
                dma(nch, 4), dma(nch, 4), dma(nch, 6), dma(nch, 6), dma(nch, 9), dma(nch, 9),
                dma(nch, 2, 4, 6), dma(nch, 2, 4, 6), dma(nch, 2, 6), dma(nch, 2, 6),
                dma(2, 8, 2), dma(2, 8, 2)]
    w = s((2, HID, DS), BF)
    return pl.pallas_call(
        functools.partial(layer_kernel, cap, chunks, table_base(plans, index)),
        out_shape=(s((OWN, DM), BF), s((1, OWN), F32), s((OWN, DM), BF), w, w, w),
        in_specs=[pl.BlockSpec(memory_space=pltpu.SMEM), vm, vm, vm, any_, any_, any_],
        out_specs=(vm,) * 6,
        scratch_shapes=scratch,
        compiler_params=pltpu.CompilerParams(
            collective_id=cid, has_side_effects=True, vmem_limit_bytes=VLIM),
        name="layer_%d_%d" % (cap, total),
    )(tab, rows, oc, rw, wg, wu, wd)


def run(rows, oc, rw, counts, tab, wg, wu, wd):
    cap, rmax = 16, ROWS + BR
    rw = rw.reshape(OWN, 1)
    xg, sg = gather_rows(cap, 0, tab, rows, oc, rw)
    part, xc, sc = first_matmuls(cap, rmax, counts, tab, xg, sg, wg, wu, wd)
    h = exchange(rmax, rmax, 1, part)
    o, gr, dg, du, dd = second_matmuls(cap, rmax, counts, tab, h, xc, sc, wg, wu, wd)
    layer_out, grad_weight, grad_rows = reduce_rows(cap, 2, tab, o, gr, rw, oc)
    return layer_out, grad_weight.reshape(1, OWN), grad_rows, dg, du, dd


def per_device(routed_rows, out_cotangent, route_weight, expert_counts, w_gate, w_up, w_down):
    rw = route_weight.reshape(1, OWN)
    wg, wu = jnp.swapaxes(w_gate, 1, 2), jnp.swapaxes(w_up, 1, 2)
    tab = plan_table(PLANS, expert_counts)
    pick = tab[table_base(PLANS, len(PLANS)), 0]

    def fast(i, rows, oc, rw, counts, tab, wg, wu, wd):
        return layer(PLANS, i, 3 + i, tab, rows, oc, rw, wg, wu, wd)

    branches = [functools.partial(fast, i) for i in range(len(PLANS))] + [run]
    layer_out, grad_weight, grad_rows, dg, du, dd = lax.switch(
        pick, branches, routed_rows, out_cotangent, rw, expert_counts, tab, wg, wu, w_down)
    return (layer_out, grad_weight.reshape(OWN), grad_rows,
            jnp.swapaxes(dg, 1, 2), jnp.swapaxes(du, 1, 2), dd)


def solution(mesh):
    return jax.shard_map(
        per_device,
        mesh=mesh,
        in_specs=(
            P(("dp", "et"), None),
            P(("dp", "et"), None),
            P(("dp", "et")),
            P(),
            P(None, None, "et"),
            P(None, None, "et"),
            P(None, "et", None),
        ),
        out_specs=(
            P(("dp", "et"), None),
            P(("dp", "et")),
            P(("dp", "et"), None),
            P(None, "dp", "et"),
            P(None, "dp", "et"),
            P(None, "et", "dp"),
        ),
        check_vma=False,
    )
```

```python
import functools

import jax
import jax.numpy as jnp
from jax import lax
from jax.experimental import pallas as pl
from jax.experimental.pallas import tpu as pltpu
from jax.sharding import PartitionSpec as P

MESH = pl.DeviceIdType.MESH
BF = jnp.bfloat16
F32 = jnp.float32
GROUPS, SLOTS, OWN, DM, HID = 8, 512, 32, 4096, 448
DS = DM // GROUPS
ROWS = GROUPS * SLOTS
H2, H3 = 2 * HID, 3 * HID
BR = 256
T = 16
TB = BR // T
PLANS = ((8, ((0, 3, 768), (3, 8, 768))), (10, ((0, 4, 1024), (4, 10, 768))))
VLIM = 60 * 1024 * 1024


def rcopy(src, dst, ssem, rsem, dev):
    return pltpu.make_async_remote_copy(
        src_ref=src, dst_ref=dst, send_sem=ssem, recv_sem=rsem,
        device_id=dev, device_id_type=MESH,
    )


def spot(g, s):
    return (s + 3 * g + 8 * (s // 16)) % 16


def origin(g, m, j):
    return 16 * m + (j + 32 - 3 * g - 8 * m) % 16


def plane(axis, pos, j):
    y, x = j // 4, j % 4
    return {"et": y * 4 + pos % 4} if axis == "x" else {"et": (pos % 4) * 4 + x}


def greet(near, others):
    bar = pltpu.get_barrier_semaphore()
    for dev in near:
        pl.semaphore_signal(bar, inc=1, device_id=dev, device_id_type=MESH)
    for dd, jj in others:
        pl.semaphore_signal(bar, inc=1, device_id={"dp": dd, "et": jj}, device_id_type=MESH)
    pl.semaphore_wait(bar, len(near) + len(others))


def deliver(me, src, dst, ssem, rsem, dd, jj):
    d, j = me
    here = jnp.logical_and(dd == d, jj == j)
    far = rcopy(src, dst, ssem, rsem, {"dp": dd, "et": jj})

    @pl.when(here)
    def _():
        pltpu.make_async_copy(src, dst, rsem).start()

    @pl.when(jnp.logical_not(here))
    def _():
        far.start()

    def finish():
        @pl.when(jnp.logical_not(here))
        def _():
            far.wait_send()

    return finish


def gather_kernel(cap, tab, rows_ref, oc_ref, rw_ref, xg, sg,
                  sc, rb0, rb1, stage, psend, precv, osem, rsend, rrecv):
    d, j = lax.axis_index("dp"), lax.axis_index("et")
    me = (d, j)
    y, x = j // 4, j % 4
    lo = cap // 2
    senders = [((d + 8 - k) % 8, origin((d + 8 - k) % 8, m, j) // 2) for k in range(8) for m in range(2)]
    greet([plane("x", x + 1, j), plane("x", x + 3, j), plane("y", y + 1, j), plane("y", y + 3, j)],
          senders)
    mm = j // 8
    rb = (rb0, rb1)
    done = []
    arrays = []
    for a, (src, out, first, second) in enumerate(
        ((rows_ref, xg, "x", "y"), (sc, sg, "y", "x"))
    ):
        if a == 1:
            sc[...] = (rw_ref[...] * oc_ref[...].astype(F32)).astype(BF)
        for k in range(8):
            dd = (d + k) % 8
            cols = pl.ds(pl.multiple_of(dd * DS, DS), DS)
            for hh in range(2):
                jj = spot(d, 2 * j + hh)
                done.append(deliver(me, src.at[pl.ds(T * hh, T), cols], rb[a].at[2 * d + mm],
                                    psend.at[a, k, hh], precv.at[a, k, mm], dd, jj))
        p, q = (x, y) if first == "x" else (y, x)

        def blk(pp, qq, half=None, out=out, first=first):
            yy, xx = (qq % 4, pp % 4) if first == "x" else (pp % 4, qq % 4)
            g = slice(None) if half is None else (pl.ds(0, lo) if half == 0 else pl.ds(lo, cap - lo))
            return out.at[yy, xx, g]

        def send(i, ref, axis, pos, a=a, own=None):
            c = rcopy(ref if own is None else own, ref, rsend.at[a, i], rrecv.at[a, i], plane(axis, pos, j))
            c.start()
            return c

        arrays.append((p, q, first, second, blk, send))

    sent = [dict(), dict()]

    def second_sends(a, u, own=None):
        p, q, first, second, blk, send = arrays[a]
        base = 4 + 4 * (u % 4)
        sent[a][base] = send(base, blk(p + u, q), second, q + 1, own=own)
        sent[a][base + 1] = send(base + 1, blk(p + u, q), second, q + 3, own=own)

    def second_forward(a, u):
        p, q, first, second, blk, send = arrays[a]
        base = 4 + 4 * (u % 4)
        sent[a][base].wait_recv()
        sent[a][base + 2] = send(base + 2, blk(p + u, q + 3, 0), second, q + 1)
        sent[a][base + 1].wait_recv()
        sent[a][base + 3] = send(base + 3, blk(p + u, q + 1, 1), second, q + 3)

    keep = []
    for a in range(2):
        p, q, first, second, blk, send = arrays[a]
        for k in range(8):
            for m in range(2):
                g = (d + 8 - k) % 8
                pltpu.make_async_copy(rb[a].at[2 * g + m], rb[a].at[2 * g + m], precv.at[a, k, m]).wait()
        for i in range(cap):
            stage[a, i] = rb[a][tab[j, i]]
        sent[a][0] = send(0, blk(p, q), first, p + 1, own=stage.at[a])
        sent[a][1] = send(1, blk(p, q), first, p + 3, own=stage.at[a])
        second_sends(a, 0, own=stage.at[a])
        c = pltpu.make_async_copy(stage.at[a], blk(p, q), osem.at[a])
        c.start()
        keep.append(c)
    for a in range(2):
        p, q, first, second, blk, send = arrays[a]
        sent[a][0].wait_recv()
        sent[a][2] = send(2, blk(p + 3, q, 0), first, p + 1)
        second_sends(a, 3)
        sent[a][1].wait_recv()
        sent[a][3] = send(3, blk(p + 1, q, 1), first, p + 3)
        second_sends(a, 1)
    for a in range(2):
        second_forward(a, 0)
    for a in range(2):
        sent[a][2].wait_recv()
        sent[a][3].wait_recv()
        second_sends(a, 2)
    for u in (3, 1, 2):
        for a in range(2):
            second_forward(a, u)
    for a in range(2):
        keep[a].wait()
        for u in range(4):
            sent[a][6 + 4 * u].wait_recv()
            sent[a][7 + 4 * u].wait_recv()
        for c in sent[a].values():
            c.wait_send()
    for f in done:
        f()


def gather_rows(cap, cid, tab, rows, oc, rw):
    shape = jax.ShapeDtypeStruct((4, 4, cap, T, DS), BF)
    vm = pl.BlockSpec(memory_space=pltpu.VMEM)
    return pl.pallas_call(
        functools.partial(gather_kernel, cap),
        out_shape=(shape, shape),
        in_specs=[pl.BlockSpec(memory_space=pltpu.SMEM), vm, vm, vm],
        out_specs=(pl.BlockSpec(memory_space=pl.ANY),) * 2,
        scratch_shapes=[
            pltpu.VMEM((OWN, DM), BF),
            pltpu.VMEM((16, T, DS), BF),
            pltpu.VMEM((16, T, DS), BF),
            pltpu.VMEM((2, cap, T, DS), BF),
            pltpu.SemaphoreType.DMA((2, 8, 2)),
            pltpu.SemaphoreType.DMA((2, 8, 2)),
            pltpu.SemaphoreType.DMA((2,)),
            pltpu.SemaphoreType.DMA((2, 20)),
            pltpu.SemaphoreType.DMA((2, 20)),
        ],
        compiler_params=pltpu.CompilerParams(
            collective_id=cid, has_side_effects=True, vmem_limit_bytes=VLIM),
        name="gather_rows_%d" % cap,
    )(tab, rows, oc, rw)


def segments(cnt):
    segs, t = [], 0
    ends = []
    for e in range(2):
        row = []
        for g in range(GROUPS):
            c = cnt[e, g]
            first = 0 if e == 0 else (cnt[0, g] + 127) // 128 * 8
            n = (c + T - 1) // T
            row.append((c, first, n, t))
            t = t + n
        ends.append(t)
        t = (t + TB - 1) // TB * TB
        ends.append(t)
        segs.append(row)
    return segs, ends


def tile(i):
    return pl.ds(pl.multiple_of(i * T, T), T)


def rows_of(b):
    return pl.ds(pl.multiple_of(b * BR, BR), BR)


def weight_copies(wg, wu, wd, wb, wsem):
    d = lax.axis_index("dp")
    cols = pl.ds(pl.multiple_of(d * DS, DS), DS)
    return [pltpu.make_async_copy(w.at[:, :, cols], wb.at[:, pl.ds(i * HID, HID), :], wsem.at[i])
            for i, w in enumerate((wg, wu, wd))]


TRANS_R = (((1,), (1,)), ((), ()))
TRANS_L = (((0,), (0,)), ((), ()))


def first_kernel(cap, cnt, tab, xg, sg, wg, wu, wd, part, xc_o, sc_o,
                 xv, sv, xc, sc, wb, pv, rsem, wsem, osem):
    segs, ends = segments(cnt)
    loads = [pltpu.make_async_copy(xg, xv, rsem.at[0]), pltpu.make_async_copy(sg, sv, rsem.at[1])]
    wcp = weight_copies(wg, wu, wd, wb, wsem)
    for c in loads + wcp:
        c.start()
    for c in loads:
        c.wait()
    zeros = jnp.zeros((T, DS), BF)
    iota = lax.broadcasted_iota(jnp.int32, (T, DS), 0)

    def source(g, s):
        jj = spot(g, s)
        return tile(jj * cap + tab[jj, 16 + 2 * g + s // 16])

    for e in range(2):
        for g in range(GROUPS):
            c, first, n, t0 = segs[e][g]

            def move(k, _, g=g, first=first, t0=t0):
                src = source(g, first + k)
                xc[tile(t0 + k), :] = xv[src, :]
                sc[tile(t0 + k), :] = sv[src, :]
                return 0

            lax.fori_loop(0, n - 1, move, 0)
            keep = iota < c - T * (n - 1)
            src = source(g, first + n - 1)
            xt = xv[src, :].astype(F32)
            st = sv[src, :].astype(F32)
            xc[tile(t0 + n - 1), :] = jnp.where(keep, xt, 0.0).astype(BF)
            sc[tile(t0 + n - 1), :] = jnp.where(keep, st, 0.0).astype(BF)

        def blank(t, _):
            xc[tile(t), :] = zeros
            sc[tile(t), :] = zeros
            return 0

        lax.fori_loop(ends[2 * e], ends[2 * e + 1], blank, 0)
    for c in wcp:
        c.wait()
    nb0, nb = ends[1] // TB, ends[3] // TB

    def out_copies(b):
        rows = rows_of(b)
        return (pltpu.make_async_copy(pv.at[rows], part.at[rows], osem.at[0]),
                pltpu.make_async_copy(xc.at[rows], xc_o.at[rows], osem.at[1]),
                pltpu.make_async_copy(sc.at[rows], sc_o.at[rows], osem.at[2]))

    def block(b, _):
        e = (b >= nb0).astype(jnp.int32)
        rows = rows_of(b)
        pv[rows, 0:H2] = lax.dot_general(
            xc[rows, :], wb[e, 0:H2, :], TRANS_R, preferred_element_type=F32).astype(BF)
        pv[rows, H2:H3] = lax.dot_general(
            sc[rows, :], wb[e, H2:H3, :], TRANS_R, preferred_element_type=F32).astype(BF)
        for c in out_copies(b):
            c.start()
        return 0

    lax.fori_loop(0, nb, block, 0)

    def drain(b, _):
        for c in out_copies(b):
            c.wait()
        return 0

    lax.fori_loop(0, nb, drain, 0)


def first_matmuls(cap, rmax, counts, tab, xg, sg, wg, wu, wd):
    any_ = pl.BlockSpec(memory_space=pl.ANY)
    sm = pl.BlockSpec(memory_space=pltpu.SMEM)
    n = 16 * cap * T
    return pl.pallas_call(
        functools.partial(first_kernel, cap),
        out_shape=(jax.ShapeDtypeStruct((rmax, H3), BF),
                   jax.ShapeDtypeStruct((rmax, DS), BF),
                   jax.ShapeDtypeStruct((rmax, DS), BF)),
        in_specs=[sm, sm] + [any_] * 5,
        out_specs=(any_,) * 3,
        scratch_shapes=[
            pltpu.VMEM((n, DS), BF), pltpu.VMEM((n, DS), BF),
            pltpu.VMEM((rmax, DS), BF), pltpu.VMEM((rmax, DS), BF),
            pltpu.VMEM((2, H3, DS), BF),
            pltpu.VMEM((rmax, H3), BF),
            pltpu.SemaphoreType.DMA((2,)), pltpu.SemaphoreType.DMA((3,)),
            pltpu.SemaphoreType.DMA((3,)),
        ],
        compiler_params=pltpu.CompilerParams(vmem_limit_bytes=VLIM),
        name="first_matmuls_%d" % cap,
    )(counts, tab, xg.reshape(n, DS), sg.reshape(n, DS), wg, wu, wd)


def exchange_kernel(r, p, h, own, prt, q, l1, r1, s1, s2, l2, r2, tot, res,
                    osem, psend, precv, bsend, brecv, gsend, grecv, lsem):
    d = lax.axis_index("dp")
    z, c = d // 2, d % 2
    r8, r16 = r // 8, r // 16
    up, down = {"dp": (z + 1) % 4 * 2 + c}, {"dp": (z + 3) % 4 * 2 + c}
    mate = {"dp": z * 2 + 1 - c}
    bar = pltpu.get_barrier_semaphore()
    for dev in (up, down, mate):
        pl.semaphore_signal(bar, inc=1, device_id=dev, device_id_type=MESH)
    pl.semaphore_wait(bar, 3)

    def rows(zz, cc):
        return pl.ds(pl.multiple_of((zz % 4 * 2 + cc) * r8, r16), r8)

    def half(zz, cc, i):
        return pl.ds(pl.multiple_of((zz % 4 * 2 + cc) * r8 + i * r16, r16), r16)

    first, second = pl.ds(0, r16), pl.ds(r16, r16)
    pair, mine = {}, {}
    for i in (2, 1, 3, 0):
        pair[i] = rcopy(p.at[rows(z + i, 1 - c)], prt.at[i], psend.at[i], precv.at[i], mate)
        pair[i].start()
        mine[i] = pltpu.make_async_copy(p.at[rows(z + i, c)], own.at[i], osem.at[i])
        mine[i].start()

    def bsum(i):
        mine[i].wait()
        pair[i].wait_recv()

        def one(k, _):
            q[i, tile(k), :] = (own[i, tile(k), :].astype(F32) + prt[i, tile(k), :].astype(F32)).astype(BF)
            return 0

        lax.fori_loop(0, r8 // T, one, 0)

    def add_rows(dst, src, i, off):
        def one(k, _):
            dst[tile(k), :] = (src[tile(k), :].astype(F32) + q[i, tile(off + k), :].astype(F32)).astype(BF)
            return 0

        lax.fori_loop(0, r16 // T, one, 0)

    cps = []

    def push(i, src, dst, dev):
        cp = rcopy(src, dst, bsend.at[i], brecv.at[i], dev)
        cp.start()
        cps.append(cp)
        return cp

    bsum(2)
    a_l = push(0, q.at[2, first], l1, up)
    a_r = push(1, q.at[2, second], r1, down)
    bsum(1)
    b_l2 = push(2, q.at[1, second], l2.at[second], up)
    bsum(3)
    b_r1 = push(3, q.at[3, first], r2.at[first], down)
    a_l.wait_recv()
    add_rows(s1, l1, 1, 0)
    b_l1 = push(4, s1, l2.at[first], up)
    a_r.wait_recv()
    add_rows(s2, r1, 3, r16 // T)
    b_r2 = push(5, s2, r2.at[second], down)
    mine[0].wait()
    pair[0].wait_recv()
    for cp in (b_l2, b_r1, b_l1, b_r2):
        cp.wait_recv()

    def final(k, _):
        t = tile(k)
        tot[...] = (own[0, t, :].astype(F32) + prt[0, t, :].astype(F32)
                    + l2[t, :].astype(F32) + r2[t, :].astype(F32))
        gate, lin, grad = tot[:, 0:HID], tot[:, HID:H2], tot[:, H2:H3]
        s = 1.0 / (1.0 + jnp.exp(-gate))
        act = gate * s
        res[t, 0:HID] = (grad * lin * s * (1.0 + gate * (1.0 - s))).astype(BF)
        res[t, HID:H2] = (grad * act).astype(BF)
        res[t, H2:H3] = (act * lin).astype(BF)
        return 0

    lax.fori_loop(0, r8 // T, final, 0)
    keep = pltpu.make_async_copy(res, h.at[rows(z, c)], lsem)
    keep.start()
    gps = {}

    def spread(i, src, dst, dev):
        cp = rcopy(src, dst, gsend.at[i], grecv.at[i], dev)
        cp.start()
        gps[i] = cp

    spread(0, res, h.at[rows(z, c)], up)
    spread(1, res, h.at[rows(z, c)], down)
    spread(2, res, h.at[rows(z, c)], mate)
    gps[0].wait_recv()
    spread(3, h.at[half(z + 3, c, 0)], h.at[half(z + 3, c, 0)], up)
    spread(4, h.at[rows(z + 3, c)], h.at[rows(z + 3, c)], mate)
    gps[1].wait_recv()
    spread(5, h.at[half(z + 1, c, 1)], h.at[half(z + 1, c, 1)], down)
    spread(6, h.at[rows(z + 1, c)], h.at[rows(z + 1, c)], mate)
    gps[3].wait_recv()
    spread(7, h.at[half(z + 2, c, 0)], h.at[half(z + 2, c, 0)], mate)
    gps[5].wait_recv()
    spread(8, h.at[half(z + 2, c, 1)], h.at[half(z + 2, c, 1)], mate)
    for i in (2, 4, 6, 7, 8):
        gps[i].wait_recv()
    keep.wait()
    for cp in list(pair.values()) + cps + list(gps.values()):
        cp.wait_send()


def exchange(r, rmax, cid, part):
    r8, r16 = r // 8, r // 16
    any_ = pl.BlockSpec(memory_space=pl.ANY)
    v = lambda *s: pltpu.VMEM(s + (H3,), BF)
    dma = lambda n: pltpu.SemaphoreType.DMA((n,))
    return pl.pallas_call(
        functools.partial(exchange_kernel, r),
        out_shape=jax.ShapeDtypeStruct((rmax, H3), BF),
        in_specs=[any_],
        out_specs=any_,
        scratch_shapes=[
            v(4, r8), v(4, r8), v(4, r8),
            v(r16), v(r16), v(r16), v(r16),
            v(r8), v(r8), pltpu.VMEM((T, H3), F32), v(r8),
            dma(4), dma(4), dma(4), dma(6), dma(6), dma(9), dma(9), pltpu.SemaphoreType.DMA,
        ],
        compiler_params=pltpu.CompilerParams(
            collective_id=cid, has_side_effects=True, vmem_limit_bytes=VLIM),
        name="exchange_%d_%d" % (cid, r),
    )(part)


def second_kernel(cap, cnt, tab, h, xc_i, sc_i, wg, wu, wd, o, gr, dg, du, dd,
                  hv, xc, sc, wb, ov, gv, au, ad, bsem, wsem):
    segs, ends = segments(cnt)
    nb0, nb = ends[1] // TB, ends[3] // TB
    wcp = weight_copies(wg, wu, wd, wb, wsem)

    def in_copies(b):
        rows = rows_of(b)
        return (pltpu.make_async_copy(h.at[rows], hv.at[rows], bsem.at[0, b]),
                pltpu.make_async_copy(xc_i.at[rows], xc.at[rows], bsem.at[1, b]),
                pltpu.make_async_copy(sc_i.at[rows], sc.at[rows], bsem.at[2, b]))

    for c in wcp:
        c.start()

    def begin(b, _):
        for c in in_copies(b):
            c.start()
        return 0

    lax.fori_loop(0, nb, begin, 0)
    au[...] = jnp.zeros_like(au)
    ad[...] = jnp.zeros_like(ad)
    for c in wcp:
        c.wait()

    def block(b, _):
        e = (b >= nb0).astype(jnp.int32)
        rows = rows_of(b)
        for c in in_copies(b):
            c.wait()
        ov[rows, :] = jnp.dot(hv[rows, H2:H3], wb[e, H2:H3, :], preferred_element_type=F32).astype(BF)
        gv[rows, :] = jnp.dot(hv[rows, 0:H2], wb[e, 0:H2, :], preferred_element_type=F32).astype(BF)
        au[e] += lax.dot_general(hv[rows, 0:H2], xc[rows, :], TRANS_L, preferred_element_type=F32)
        ad[e] += lax.dot_general(hv[rows, H2:H3], sc[rows, :], TRANS_L, preferred_element_type=F32)
        return 0

    lax.fori_loop(0, nb, block, 0)
    dg[...] = au[:, 0:HID, :].astype(BF)
    du[...] = au[:, HID:H2, :].astype(BF)
    dd[...] = ad[...].astype(BF)

    for e in range(2):
        for g in range(GROUPS):
            c, first, n, t0 = segs[e][g]

            def move(k, _, g=g, first=first, t0=t0):
                s = first + k
                jj = spot(g, s)
                dst = tile(jj * cap + tab[jj, 16 + 2 * g + s // 16])
                o[dst, :] = ov[tile(t0 + k), :]
                gr[dst, :] = gv[tile(t0 + k), :]
                return 0

            lax.fori_loop(0, n, move, 0)


def second_matmuls(cap, rmax, counts, tab, h, xc, sc, wg, wu, wd):
    any_ = pl.BlockSpec(memory_space=pl.ANY)
    sm = pl.BlockSpec(memory_space=pltpu.SMEM)
    vm = pl.BlockSpec(memory_space=pltpu.VMEM)
    s = jax.ShapeDtypeStruct
    n = 16 * cap * T
    return pl.pallas_call(
        functools.partial(second_kernel, cap),
        out_shape=(s((n, DS), BF), s((n, DS), BF)) + (s((2, HID, DS), BF),) * 3,
        in_specs=[sm, sm] + [any_] * 6,
        out_specs=(vm,) * 5,
        scratch_shapes=[
            pltpu.VMEM((rmax, H3), BF),
            pltpu.VMEM((rmax, DS), BF), pltpu.VMEM((rmax, DS), BF),
            pltpu.VMEM((2, H3, DS), BF),
            pltpu.VMEM((rmax, DS), BF), pltpu.VMEM((rmax, DS), BF),
            pltpu.VMEM((2, H2, DS), F32), pltpu.VMEM((2, HID, DS), F32),
            pltpu.SemaphoreType.DMA((3, rmax // BR)), pltpu.SemaphoreType.DMA((3,)),
        ],
        compiler_params=pltpu.CompilerParams(vmem_limit_bytes=VLIM),
        name="second_matmuls_%d" % cap,
    )(counts, tab, h, xc, sc, wg, wu, wd)


def reduce_kernel(cap, tab, o_ref, g_ref, rw_ref, oc_ref, out_o, out_w, out_g,
                  l1, r1, s1, s2, l2, r2, acc, bl1, br1, bs1, bs2, bl2, br2, fin, ex, rec,
                  asend, arecv, bsend, brecv, psend, precv):
    d, j = lax.axis_index("dp"), lax.axis_index("et")
    me = (d, j)
    y, x = j // 4, j % 4
    owners = [((d + k) % 8, spot(d, 2 * j + hh)) for k in range(8) for hh in range(2)]
    greet([plane("x", x + 1, j), plane("x", x + 3, j), plane("y", y + 1, j), plane("y", y + 3, j)],
          owners)
    half = cap // 2
    lo, hi = pl.ds(0, half), pl.ds(half, cap - half)
    order = (2, 1, 3, 0)
    info = []
    cps = []
    for a, (src, first) in enumerate(((o_ref, "y"), (g_ref, "x"))):
        second = "x" if first == "y" else "y"
        p, q = (y, x) if first == "y" else (x, y)

        def blk(pp, qq, g, src=src, first=first):
            yy, xx = (pp % 4, qq % 4) if first == "y" else (qq % 4, pp % 4)
            return src.at[yy, xx, g]

        info.append((p, q, first, second, blk))

    def push(sems, key, src, dst, axis, pos):
        send, recv = sems
        cp = rcopy(src, dst, send.at[key], recv.at[key], plane(axis, pos, j))
        cp.start()
        cps.append(cp)
        return cp

    def add2(dst, b, c):
        for g in range(half):
            dst[g] = (b[g].astype(F32) + c[g].astype(F32)).astype(BF)

    A, B = (asend, arecv), (bsend, brecv)
    av = [dict(), dict()]
    for u in order:
        for a in range(2):
            p, q, first, second, blk = info[a]
            av[a][u, 0] = push(A, (a, u, 0), blk(p + 2, q + u, lo), l1.at[a, u], first, p + 1)
            av[a][u, 1] = push(A, (a, u, 1), blk(p + 2, q + u, hi), r1.at[a, u], first, p + 3)
            av[a][u, 2] = push(A, (a, u, 2), blk(p + 1, q + u, hi), l2.at[a, u, hi], first, p + 1)
            av[a][u, 3] = push(A, (a, u, 3), blk(p + 3, q + u, lo), r2.at[a, u, lo], first, p + 3)
    for u in order:
        for a in range(2):
            p, q, first, second, blk = info[a]
            av[a][u, 0].wait_recv()
            add2(s1.at[a, u], l1.at[a, u], blk(p + 1, q + u, lo))
            av[a][u, 4] = push(A, (a, u, 4), s1.at[a, u], l2.at[a, u, lo], first, p + 1)
            av[a][u, 1].wait_recv()
            add2(s2.at[a, u], r1.at[a, u], blk(p + 3, q + u, hi))
            av[a][u, 5] = push(A, (a, u, 5), s2.at[a, u], r2.at[a, u, hi], first, p + 3)
    bv = [dict(), dict()]
    for u in order:
        for a in range(2):
            p, q, first, second, blk = info[a]
            for i in (2, 3, 4, 5):
                av[a][u, i].wait_recv()
            mine = blk(p, q + u, pl.ds(0, cap))
            for g in range(cap):
                acc[a, u, g] = (mine[g].astype(F32) + l2[a, u, g].astype(F32)
                                + r2[a, u, g].astype(F32)).astype(BF)
            if u == 2:
                bv[a][0] = push(B, (a, 0), acc.at[a, 2, lo], bl1.at[a], second, q + 1)
                bv[a][1] = push(B, (a, 1), acc.at[a, 2, hi], br1.at[a], second, q + 3)
            elif u == 1:
                bv[a][2] = push(B, (a, 2), acc.at[a, 1, hi], bl2.at[a, hi], second, q + 1)
            elif u == 3:
                bv[a][3] = push(B, (a, 3), acc.at[a, 3, lo], br2.at[a, lo], second, q + 3)
    for a in range(2):
        p, q, first, second, blk = info[a]
        bv[a][0].wait_recv()
        add2(bs1.at[a], bl1.at[a], acc.at[a, 1, lo])
        bv[a][4] = push(B, (a, 4), bs1.at[a], bl2.at[a, lo], second, q + 1)
        bv[a][1].wait_recv()
        add2(bs2.at[a], br1.at[a], acc.at[a, 3, hi])
        bv[a][5] = push(B, (a, 5), bs2.at[a], br2.at[a, hi], second, q + 3)
    done = []
    for a in range(2):
        for i in (2, 3, 4, 5):
            bv[a][i].wait_recv()
        for g in range(cap):
            fin[a, g] = (acc[a, 0, g].astype(F32) + bl2[a, g].astype(F32)
                         + br2[a, g].astype(F32)).astype(BF)
        for k in range(8):
            g = (d + k) % 8
            for m in range(2):
                s = origin(g, m, j)
                at = tab[j, 16 + 2 * g + m]
                got = fin[a, jnp.maximum(at, 0)].astype(F32)
                ex[a, k, m] = jnp.where(at >= 0, got, 0.0).astype(BF)
                done.append(deliver(me, ex.at[a, k, m], rec.at[a, d, s % 2],
                                    psend.at[a, k, m], precv.at[a, k, s % 2], g, s // 2))
    for a in range(2):
        for k in range(8):
            for hh in range(2):
                spot_ref = rec.at[a, (d + 8 - k) % 8, hh]
                pltpu.make_async_copy(spot_ref, spot_ref, precv.at[a, k, hh]).wait()
    rw = rw_ref[...]
    total = jnp.zeros((OWN, 1), F32)
    for k in range(8):
        cols = slice(k * DS, (k + 1) * DS)
        comb = rec[0, k].astype(F32).reshape(OWN, DS)
        out_o[:, cols] = (rw * comb).astype(BF)
        total = total + jnp.sum(oc_ref[:, cols].astype(F32) * comb, axis=1, keepdims=True)
        out_g[:, cols] = rec[1, k].reshape(OWN, DS)
    out_w[...] = total
    for cp in cps:
        cp.wait_send()
    for f in done:
        f()


def reduce_rows(cap, cid, tab, o, g, rw, oc):
    vm = pl.BlockSpec(memory_space=pltpu.VMEM)
    s = jax.ShapeDtypeStruct
    v = lambda *sh: pltpu.VMEM(sh + (T, DS), BF)
    dma = lambda *n: pltpu.SemaphoreType.DMA(n)
    h = cap // 2
    return pl.pallas_call(
        functools.partial(reduce_kernel, cap),
        out_shape=(s((OWN, DM), BF), s((OWN, 1), F32), s((OWN, DM), BF)),
        in_specs=[pl.BlockSpec(memory_space=pltpu.SMEM)] + [vm] * 4,
        out_specs=(vm,) * 3,
        scratch_shapes=[
            v(2, 4, h), v(2, 4, h), v(2, 4, h), v(2, 4, h), v(2, 4, cap), v(2, 4, cap), v(2, 4, cap),
            v(2, h), v(2, h), v(2, h), v(2, h), v(2, cap), v(2, cap), v(2, cap),
            v(2, 8, 2), v(2, 8, 2),
            dma(2, 4, 6), dma(2, 4, 6), dma(2, 6), dma(2, 6), dma(2, 8, 2), dma(2, 8, 2),
        ],
        compiler_params=pltpu.CompilerParams(
            collective_id=cid, has_side_effects=True, vmem_limit_bytes=VLIM),
        name="reduce_rows_%d" % cap,
    )(tab, o.reshape(4, 4, cap, T, DS), g.reshape(4, 4, cap, T, DS), rw, oc)


def plan_kernel(plans, cnt, out):
    i32 = lambda v: v.astype(jnp.int32)
    f = lambda v: v.astype(F32)
    j = lax.broadcasted_iota(jnp.int32, (16, 16), 0)
    q = lax.broadcasted_iota(jnp.int32, (16, 16), 1)
    g, m = q // 2, q % 2
    s = origin(g, m, j)
    c0 = jnp.zeros((16, 16), jnp.int32)
    c1 = jnp.zeros((16, 16), jnp.int32)
    for k in range(GROUPS):
        c0 = jnp.where(g == k, cnt[0, k], c0)
        c1 = jnp.where(g == k, cnt[1, k], c1)
    s1 = (c0 + 127) // 128 * 8
    left0 = jnp.clip(c0 - T * s, 0, T)
    left1 = jnp.where(s >= s1, jnp.clip(c1 - T * (s - s1), 0, T), 0)
    live = left0 + left1 > 0
    one = f(i32(live))
    mm = lambda a, b, dims: lax.dot_general(a, b, (dims, ((), ())), preferred_element_type=F32)
    rank = mm(one, f(i32(j < q)), ((1,), (0,)))
    place = jnp.where(live, i32(rank), -1)
    orders = jnp.zeros((16, 16), jnp.int32)
    rows0 = jnp.zeros((16, 16), jnp.int32)
    rows1 = jnp.zeros((16, 16), jnp.int32)
    for k in range(16):
        hit = place == k
        pick = lambda v: jnp.sum(f(jnp.where(hit, v, 0)), axis=1, keepdims=True)
        orders = jnp.where(q == k, i32(pick(q)), orders)
        rows0 = jnp.where(q == k, i32(pick(left0)), rows0)
        rows1 = jnp.where(q == k, i32(pick(left1)), rows1)
    out[...] = jnp.zeros_like(out)
    out[0:16, 0:16] = orders
    out[0:16, 16:32] = place
    nrow = mm(jnp.ones((8, 16), F32), one, ((1,), (1,)))[0:1, :]
    ok = []
    col0 = 32
    for cap, chunks in plans:
        fits = jnp.max(nrow) <= cap
        for lo, hi, r in chunks:
            nt = r // T
            n = jnp.clip(nrow - lo, 0.0, float(hi - lo))
            n8 = jnp.broadcast_to(n, (8, 16))
            off = mm(n8, f(i32(j < q)), ((1,), (0,)))[0:1, :]
            t = lax.broadcasted_iota(jnp.int32, (nt, 16), 0)
            qq = lax.broadcasted_iota(jnp.int32, (nt, 16), 1)
            offb, nb = jnp.broadcast_to(off, (nt, 16)), jnp.broadcast_to(n, (nt, 16))
            hot = f(i32((f(t) >= offb) & (f(t) < offb + nb)))
            at = jnp.sum(hot * (f(t) - offb), axis=1, keepdims=True)
            dev = jnp.sum(hot * f(qq), axis=1, keepdims=True)
            used = jnp.sum(hot, axis=1, keepdims=True)
            col = f(i32(f(qq) == at + float(lo)))
            sel = lambda v: jnp.sum(col * mm(hot, f(v), ((1,), (0,))), axis=1, keepdims=True) * used
            for i, v in enumerate((dev * float(hi - lo) + at, sel(rows0), sel(rows1))):
                out[0:nt, col0 + i:col0 + i + 1] = i32(v)
            ncol = jnp.clip(jnp.sum(one, axis=1, keepdims=True) - lo, 0.0, float(hi - lo))
            ocol = mm(f(i32(q < j)), jnp.broadcast_to(ncol, (16, 8)), ((1,), (0,)))[:, 0:1]
            back = jnp.clip(i32(ocol) + q - lo, 0, nt - 1)
            out[0:16, col0 + 4:col0 + 20] = back + jnp.where(rows1 > 0, nt, 0)
            col0 += 20
            fits = jnp.logical_and(fits, jnp.sum(n) <= nt)
        ok.append(fits)
    level = jnp.int32(len(plans))
    for i in range(len(plans) - 1, -1, -1):
        level = jnp.where(ok[i], i, level)
    lane = lax.broadcasted_iota(jnp.int32, (8, 128), 1)
    out[0:8, :] = jnp.where(lane == 127, level, out[0:8, :])


def plan_table(plans, counts):
    return pl.pallas_call(
        functools.partial(plan_kernel, plans),
        out_shape=jax.ShapeDtypeStruct((64, 128), jnp.int32),
        in_specs=[pl.BlockSpec(memory_space=pltpu.SMEM)],
        out_specs=pl.BlockSpec(memory_space=pltpu.VMEM),
        name="tile_plan",
    )(counts)


def layer_kernel(cap, chunks, base, tab, rows_ref, oc_ref, rw_ref, wg, wu, wd,
                 out_o, out_w, out_g, dg, du, dd_o, sc, rb0, rb1, stage, wcat, xcat, scat, hall,
                 ov, gv, fin, ex, rec, *rest):
    d, j = lax.axis_index("dp"), lax.axis_index("et")
    me = (d, j)
    y, x = j // 4, j % 4
    z, c = d // 2, d % 2
    nch = len(chunks)
    names = ("xg", "sg", "part", "prt", "q", "zl1", "zr1", "zs1", "zs2", "zl2", "zr2", "tot",
             "ob", "gb", "l1", "r1", "s1", "s2", "l2", "r2", "acc", "bl1", "br1", "bs1", "bs2", "bl2", "br2")
    buf = [dict(zip(names, rest[i * len(names):(i + 1) * len(names)])) for i in range(nch)]
    (psend, precv, wsem, rsend, rrecv, zps, zpr, zbs, zbr, zgs, zgr,
     asend, arecv, bsend, brecv, qsend, qrecv) = rest[nch * len(names):]
    up, down = {"dp": (z + 1) % 4 * 2 + c}, {"dp": (z + 3) % 4 * 2 + c}
    mate = {"dp": z * 2 + 1 - c}
    senders = [((d + 8 - k) % 8, origin((d + 8 - k) % 8, m, j) // 2) for k in range(8) for m in range(2)]
    greet([plane("x", x + 1, j), plane("x", x + 3, j), plane("y", y + 1, j), plane("y", y + 3, j),
           up, down, mate], senders)
    finish = []
    rb = (rb0, rb1)
    offs = []
    for i in range(nch):
        offs.append(base + 20 * i)
    first_row = [sum(r for _, _, r in chunks[:i]) for i in range(nch)]

    def remote(src, dst, ssem, rsem, dev):
        cp = rcopy(src, dst, ssem, rsem, dev)
        cp.start()
        finish.append(cp.wait_send)
        return cp

    mm = j // 8
    cols = pl.ds(pl.multiple_of(d * DS, DS), DS)
    wcp = []
    for a, src in enumerate((rows_ref, sc)):
        if a == 1:
            eye = lax.broadcasted_iota(jnp.int32, (OWN, OWN), 0) == lax.broadcasted_iota(jnp.int32, (OWN, OWN), 1)
            rw = jnp.sum(jnp.where(eye, jnp.broadcast_to(rw_ref[...], (OWN, OWN)), 0.0), axis=1, keepdims=True)
            for k in range(8):
                cs = slice(k * DS, (k + 1) * DS)
                sc[:, cs] = (rw * oc_ref[:, cs].astype(F32)).astype(BF)
        for k in range(8):
            dd = (d + k) % 8
            cs = pl.ds(pl.multiple_of(dd * DS, DS), DS)
            for hh in range(2):
                jj = spot(d, 2 * j + hh)
                finish.append(deliver(me, src.at[pl.ds(T * hh, T), cs], rb[a].at[2 * d + mm],
                                      psend.at[a, k, hh], precv.at[a, k, mm], dd, jj))
    for e in range(2):
        for i, w in enumerate((wg, wu, wd)):
            cp = pltpu.make_async_copy(w.at[e, :, cols],
                                       wcat.at[pl.ds(i * HID, HID), pl.ds(e * DS, DS)], wsem.at[e, i])
            cp.start()
            wcp.append(cp)

    def arrive(a):
        for k in range(8):
            for m in range(2):
                ref = rb[a].at[2 * ((d + 8 - k) % 8) + m]
                pltpu.make_async_copy(ref, ref, precv.at[a, k, m]).wait()
        for i in range(cap):
            stage[a, i] = rb[a][tab[j, i]]

    def gather(ch):
        lo, hi, r = chunks[ch]
        nt = hi - lo
        h0 = nt // 2
        ax = (("x", "y", x, y), ("y", "x", y, x))
        outs = (buf[ch]["xg"], buf[ch]["sg"])

        def blk(a, pp, qq, half=None):
            yy, xx = (qq % 4, pp % 4) if a == 0 else (pp % 4, qq % 4)
            off, n = (0, nt) if half is None else ((0, h0) if half == 0 else (h0, nt - h0))
            return outs[a].at[pl.ds((4 * yy + xx) * nt + off, n)]

        sent = [dict(), dict()]

        def send(a, i, ref, axis, pos, own=None):
            sent[a][i] = remote(ref if own is None else own, ref, rsend.at[ch, a, i], rrecv.at[ch, a, i],
                                plane(axis, pos, j))

        def seconds(a, u, own=None):
            first, second, p, q = ax[a]
            i = 4 + 4 * (u % 4)
            send(a, i, blk(a, p + u, q), second, q + 1, own)
            send(a, i + 1, blk(a, p + u, q), second, q + 3, own)

        def forward(a, u):
            first, second, p, q = ax[a]
            i = 4 + 4 * (u % 4)
            sent[a][i].wait_recv()
            send(a, i + 2, blk(a, p + u, q + 3, 0), second, q + 1)
            sent[a][i + 1].wait_recv()
            send(a, i + 3, blk(a, p + u, q + 1, 1), second, q + 3)

        for a in range(2):
            first, second, p, q = ax[a]
            if ch == 0:
                arrive(a)
            own = stage.at[a, pl.ds(lo, nt)]
            send(a, 0, blk(a, p, q), first, p + 1, own)
            send(a, 1, blk(a, p, q), first, p + 3, own)
            seconds(a, 0, own)
            outs[a][pl.ds(j * nt, nt)] = stage[a, lo:hi]
        yield
        for a in range(2):
            first, second, p, q = ax[a]
            sent[a][0].wait_recv()
            send(a, 2, blk(a, p + 3, q, 0), first, p + 1)
            seconds(a, 3)
            sent[a][1].wait_recv()
            send(a, 3, blk(a, p + 1, q, 1), first, p + 3)
            seconds(a, 1)
            yield
        for a in range(2):
            forward(a, 0)
            yield
        for a in range(2):
            sent[a][2].wait_recv()
            sent[a][3].wait_recv()
            seconds(a, 2)
        yield
        for u in (3, 1, 2):
            for a in range(2):
                forward(a, u)
            yield
        for a in range(2):
            for u in range(4):
                sent[a][6 + 4 * u].wait_recv()
                sent[a][7 + 4 * u].wait_recv()

    def first(ch):
        lo, hi, r = chunks[ch]
        xg, sg, part = buf[ch]["xg"], buf[ch]["sg"], buf[ch]["part"]
        iota = lax.broadcasted_iota(jnp.int32, (T, DS), 0)
        r0 = first_row[ch]

        def pack(t, _):
            src = tab[t, offs[ch]]
            xt, st = xg[src].astype(F32), sg[src].astype(F32)
            dst = tile(r0 // T + t)
            for e in range(2):
                keep = iota < tab[t, offs[ch] + 1 + e]
                cs = slice(e * DS, (e + 1) * DS)
                xcat[dst, cs] = jnp.where(keep, xt, 0.0).astype(BF)
                scat[dst, cs] = jnp.where(keep, st, 0.0).astype(BF)
            return 0

        lax.fori_loop(0, r // T, pack, 0)
        if ch == 0:
            for cp in wcp:
                cp.wait()

        def mul(i, _):
            src = pl.ds(pl.multiple_of(r0 + i * BR, BR), BR)
            dst = rows_of(i)
            part[dst, 0:H2] = lax.dot_general(
                xcat[src, :], wcat[0:H2, :], TRANS_R, preferred_element_type=F32).astype(BF)
            part[dst, H2:H3] = lax.dot_general(
                scat[src, :], wcat[H2:H3, :], TRANS_R, preferred_element_type=F32).astype(BF)
            return 0

        lax.fori_loop(0, r // BR, mul, 0)

    def exchange_chunk(ch):
        lo, hi, r = chunks[ch]
        bf = buf[ch]
        part, prt, q, tot = bf["part"], bf["prt"], bf["q"], bf["tot"]
        r8, r16 = r // 8, r // 16
        r0 = first_row[ch]
        fst, snd = pl.ds(0, r16), pl.ds(r16, r16)

        def rows(zz, cc, off=0, n=None):
            return pl.ds(pl.multiple_of((zz % 4 * 2 + cc) * r8 + off, 16), r8 if n is None else n)

        def hrows(zz, cc, off=0, n=None):
            return hall.at[pl.ds(pl.multiple_of(r0 + (zz % 4 * 2 + cc) * r8 + off, 16), r8 if n is None else n)]

        pair = {}
        for i in (2, 1, 3, 0):
            pair[i] = remote(part.at[rows(z + i, 1 - c)], prt.at[i], zps.at[ch, i], zpr.at[ch, i], mate)
        yield

        def bsum(i):
            pair[i].wait_recv()
            start = (z + i) % 4 * 2 + c

            def one(k, _):
                src = pl.ds(pl.multiple_of(start * r8 + k * T, T), T)
                q[i, tile(k), :] = (part[src, :].astype(F32) + prt[i, tile(k), :].astype(F32)).astype(BF)
                return 0

            lax.fori_loop(0, r8 // T, one, 0)

        def add_rows(dst, src, i, off):
            def one(k, _):
                dst[tile(k), :] = (src[tile(k), :].astype(F32) + q[i, tile(off + k), :].astype(F32)).astype(BF)
                return 0

            lax.fori_loop(0, r16 // T, one, 0)

        def push(i, src, dst, dev):
            return remote(src, dst, zbs.at[ch, i], zbr.at[ch, i], dev)

        bsum(2)
        a_l = push(0, q.at[2, fst], bf["zl1"], up)
        a_r = push(1, q.at[2, snd], bf["zr1"], down)
        bsum(1)
        b_l2 = push(2, q.at[1, snd], bf["zl2"].at[snd], up)
        bsum(3)
        b_r1 = push(3, q.at[3, fst], bf["zr2"].at[fst], down)
        yield
        a_l.wait_recv()
        add_rows(bf["zs1"], bf["zl1"], 1, 0)
        b_l1 = push(4, bf["zs1"], bf["zl2"].at[fst], up)
        a_r.wait_recv()
        add_rows(bf["zs2"], bf["zr1"], 3, r16 // T)
        b_r2 = push(5, bf["zs2"], bf["zr2"].at[snd], down)
        yield
        pair[0].wait_recv()
        for cp in (b_l2, b_r1, b_l1, b_r2):
            cp.wait_recv()
        mine = (z * 2 + c) * r8

        def final(k, _):
            t = tile(k)
            src = pl.ds(pl.multiple_of(mine + k * T, T), T)
            dst = pl.ds(pl.multiple_of(r0 + mine + k * T, T), T)
            tot[...] = (part[src, :].astype(F32) + prt[0, t, :].astype(F32)
                        + bf["zl2"][t, :].astype(F32) + bf["zr2"][t, :].astype(F32))
            gate, lin, grad = tot[:, 0:HID], tot[:, HID:H2], tot[:, H2:H3]
            s = 1.0 / (1.0 + jnp.exp(-gate))
            act = gate * s
            hall[dst, 0:HID] = (grad * lin * s * (1.0 + gate * (1.0 - s))).astype(BF)
            hall[dst, HID:H2] = (grad * act).astype(BF)
            hall[dst, H2:H3] = (act * lin).astype(BF)
            return 0

        lax.fori_loop(0, r8 // T, final, 0)
        gps = {}

        def spread(i, ref, dev):
            gps[i] = remote(ref, ref, zgs.at[ch, i], zgr.at[ch, i], dev)

        spread(0, hrows(z, c), up)
        spread(1, hrows(z, c), down)
        spread(2, hrows(z, c), mate)
        yield
        gps[0].wait_recv()
        spread(3, hrows(z + 3, c, 0, r16), up)
        spread(4, hrows(z + 3, c), mate)
        gps[1].wait_recv()
        spread(5, hrows(z + 1, c, r16, r16), down)
        spread(6, hrows(z + 1, c), mate)
        yield
        gps[3].wait_recv()
        spread(7, hrows(z + 2, c, 0, r16), mate)
        gps[5].wait_recv()
        spread(8, hrows(z + 2, c, r16, r16), mate)
        yield
        for i in (2, 4, 6, 7, 8):
            gps[i].wait_recv()

    def second(ch):
        lo, hi, r = chunks[ch]
        nt = hi - lo
        r0 = first_row[ch]
        ob, gb = buf[ch]["ob"], buf[ch]["gb"]

        def mul(i, _):
            src = pl.ds(pl.multiple_of(r0 + i * BR, BR), BR)
            for e in range(2):
                dst = pl.ds(e * (r // T) + i * TB, TB)
                cs = slice(e * DS, (e + 1) * DS)
                to = jnp.dot(hall[src, H2:H3], wcat[H2:H3, cs], preferred_element_type=F32).astype(BF)
                tg = jnp.dot(hall[src, 0:H2], wcat[0:H2, cs], preferred_element_type=F32).astype(BF)
                ov[dst] = to.reshape(TB, T, DS)
                gv[dst] = tg.reshape(TB, T, DS)
            return 0

        lax.fori_loop(0, r // BR, mul, 0)

        def unpack(jj, _):
            for i in range(nt):
                src = tab[jj, offs[ch] + 4 + lo + i]
                ob[jj, i] = ov[src]
                gb[jj, i] = gv[src]
            return 0

        lax.fori_loop(0, 16, unpack, 0)

    def reduce_chunk(ch):
        lo_t, hi_t, r = chunks[ch]
        nt = hi_t - lo_t
        h0 = nt // 2
        bf = buf[ch]
        lo, hi = pl.ds(0, h0), pl.ds(h0, nt - h0)
        srcs = (bf["ob"], bf["gb"])
        ax = (("y", "x", y, x), ("x", "y", x, y))
        order = (2, 1, 3, 0)

        def blk(a, pp, qq, g):
            yy, xx = (pp % 4, qq % 4) if a == 0 else (qq % 4, pp % 4)
            return srcs[a].at[4 * yy + xx, g]

        def push(sems, key, src, dst, axis, pos):
            return remote(src, dst, sems[0].at[(ch,) + key], sems[1].at[(ch,) + key], plane(axis, pos, j))

        def add2(n, dst, b, cc):
            for g in range(n):
                dst[g] = (b[g].astype(F32) + cc[g].astype(F32)).astype(BF)

        A, B = (asend, arecv), (bsend, brecv)
        av, bv = [dict(), dict()], [dict(), dict()]
        l1, r1, s1, s2, l2, r2, acc = (bf[k] for k in ("l1", "r1", "s1", "s2", "l2", "r2", "acc"))
        bl1, br1, bs1, bs2, bl2, br2 = (bf[k] for k in ("bl1", "br1", "bs1", "bs2", "bl2", "br2"))
        for u in order:
            for a in range(2):
                fx, sx, p, q = ax[a]
                av[a][u, 0] = push(A, (a, u, 0), blk(a, p + 2, q + u, lo), l1.at[a, u], fx, p + 1)
                av[a][u, 1] = push(A, (a, u, 1), blk(a, p + 2, q + u, hi), r1.at[a, u], fx, p + 3)
                av[a][u, 2] = push(A, (a, u, 2), blk(a, p + 1, q + u, hi), l2.at[a, u, hi], fx, p + 1)
                av[a][u, 3] = push(A, (a, u, 3), blk(a, p + 3, q + u, lo), r2.at[a, u, lo], fx, p + 3)
        yield
        for u in order:
            for a in range(2):
                fx, sx, p, q = ax[a]
                av[a][u, 0].wait_recv()
                add2(h0, s1.at[a, u], l1.at[a, u], blk(a, p + 1, q + u, lo))
                av[a][u, 4] = push(A, (a, u, 4), s1.at[a, u], l2.at[a, u, lo], fx, p + 1)
                av[a][u, 1].wait_recv()
                add2(nt - h0, s2.at[a, u], r1.at[a, u], blk(a, p + 3, q + u, hi))
                av[a][u, 5] = push(A, (a, u, 5), s2.at[a, u], r2.at[a, u, hi], fx, p + 3)
            if u in (1, 0):
                yield
        for u in order:
            for a in range(2):
                fx, sx, p, q = ax[a]
                for i in (2, 3, 4, 5):
                    av[a][u, i].wait_recv()
                mine = blk(a, p, q + u, pl.ds(0, nt))
                for g in range(nt):
                    acc[a, u, g] = (mine[g].astype(F32) + l2[a, u, g].astype(F32)
                                    + r2[a, u, g].astype(F32)).astype(BF)
                if u == 2:
                    bv[a][0] = push(B, (a, 0), acc.at[a, 2, lo], bl1.at[a], sx, q + 1)
                    bv[a][1] = push(B, (a, 1), acc.at[a, 2, hi], br1.at[a], sx, q + 3)
                elif u == 1:
                    bv[a][2] = push(B, (a, 2), acc.at[a, 1, hi], bl2.at[a, hi], sx, q + 1)
                elif u == 3:
                    bv[a][3] = push(B, (a, 3), acc.at[a, 3, lo], br2.at[a, lo], sx, q + 3)
            if u in (1, 0):
                yield
        for a in range(2):
            fx, sx, p, q = ax[a]
            bv[a][0].wait_recv()
            add2(h0, bs1.at[a], bl1.at[a], acc.at[a, 1, lo])
            bv[a][4] = push(B, (a, 4), bs1.at[a], bl2.at[a, lo], sx, q + 1)
            bv[a][1].wait_recv()
            add2(nt - h0, bs2.at[a], br1.at[a], acc.at[a, 3, hi])
            bv[a][5] = push(B, (a, 5), bs2.at[a], br2.at[a, hi], sx, q + 3)
        yield
        for a in range(2):
            for i in (2, 3, 4, 5):
                bv[a][i].wait_recv()
            for g in range(nt):
                fin[a, lo_t + g] = (acc[a, 0, g].astype(F32) + bl2[a, g].astype(F32)
                                    + br2[a, g].astype(F32)).astype(BF)

    def weight_grads():
        n = 256

        def one(i, _):
            cs = pl.ds(pl.multiple_of(i * n, n), n)
            e, os = i // (DS // n), pl.ds(pl.multiple_of(i % (DS // n) * n, n), n)
            both = lax.dot_general(hall[:, 0:H2], xcat[:, cs], TRANS_L, preferred_element_type=F32)
            dg[e, :, os] = both[0:HID].astype(BF)
            du[e, :, os] = both[HID:H2].astype(BF)
            dd_o[e, :, os] = lax.dot_general(hall[:, H2:H3], scat[:, cs], TRANS_L,
                                             preferred_element_type=F32).astype(BF)
            return 0

        lax.fori_loop(0, 2 * DS // n, one, 0)

    def drain(gen):
        for _ in gen:
            pass

    def step(gen, n=1):
        for _ in range(n):
            if next(gen, 0) == 0:
                return False
        return True

    drain(gather(0))
    first(0)
    if nch == 2:
        za, nx = exchange_chunk(0), gather(1)
        for n in (1, 3, 3, 0):
            step(za)
            step(nx, n)
        drain(nx)
        first(1)
        zb = exchange_chunk(1)
        step(zb)
        step(za)
        step(za)
        step(zb)
        drain(za)
        second(0)
        ra = reduce_chunk(0)
        step(ra)
        for n in (1, 2, 1, 2):
            step(zb)
            step(ra, n)
        drain(zb)
        second(1)
        rl = reduce_chunk(1)
        step(rl)
        drain(ra)
    else:
        drain(exchange_chunk(0))
        second(0)
        rl = reduce_chunk(0)
        step(rl)
    weight_grads()
    drain(rl)

    for a in range(2):
        for k in range(8):
            g = (d + k) % 8
            for m in range(2):
                s = origin(g, m, j)
                at = tab[j, 16 + 2 * g + m]
                got = fin[a, jnp.maximum(at, 0)].astype(F32)
                ex[a, k, m] = jnp.where(at >= 0, got, 0.0).astype(BF)
                finish.append(deliver(me, ex.at[a, k, m], rec.at[a, d, s % 2],
                                      qsend.at[a, k, m], qrecv.at[a, k, s % 2], g, s // 2))
    total = jnp.zeros((OWN, 1), F32)
    for a in range(2):
        for k in range(8):
            for hh in range(2):
                ref = rec.at[a, (d + 8 - k) % 8, hh]
                pltpu.make_async_copy(ref, ref, qrecv.at[a, k, hh]).wait()
        for k in range(8):
            cs = slice(k * DS, (k + 1) * DS)
            if a == 0:
                comb = rec[0, k].astype(F32).reshape(OWN, DS)
                out_o[:, cs] = (rw * comb).astype(BF)
                total = total + jnp.sum(oc_ref[:, cs].astype(F32) * comb, axis=1, keepdims=True)
            else:
                out_g[:, cs] = rec[1, k].reshape(OWN, DS)
    out_w[...] = jnp.sum(jnp.where(eye, jnp.broadcast_to(total, (OWN, OWN)), 0.0), axis=0, keepdims=True)
    for f in finish:
        f()


def layer(plans, index, cid, tab, rows, oc, rw, wg, wu, wd):
    cap, chunks = plans[index]
    vm = pl.BlockSpec(memory_space=pltpu.VMEM)
    any_ = pl.BlockSpec(memory_space=pl.ANY)
    s = jax.ShapeDtypeStruct
    v = lambda *sh: pltpu.VMEM(sh, BF)
    tl = lambda *sh: pltpu.VMEM(sh + (T, DS), BF)
    dma = lambda *n: pltpu.SemaphoreType.DMA(n)
    total = sum(r for _, _, r in chunks)
    rbig = max(r for _, _, r in chunks)
    nch = len(chunks)
    scratch = [v(OWN, DM), tl(16), tl(16), tl(2, cap), v(H3, 2 * DS), v(total, 2 * DS), v(total, 2 * DS),
               v(total, H3), tl(2 * rbig // T), tl(2 * rbig // T), tl(2, cap), tl(2, 8, 2), tl(2, 8, 2)]
    for lo, hi, r in chunks:
        nt = hi - lo
        h0, h1 = nt // 2, nt - nt // 2
        r8, r16 = r // 8, r // 16
        scratch += [tl(16 * nt), tl(16 * nt), v(r, H3), v(4, r8, H3), v(4, r8, H3),
                    v(r16, H3), v(r16, H3), v(r16, H3), v(r16, H3), v(r8, H3), v(r8, H3),
                    pltpu.VMEM((T, H3), F32), tl(16, nt), tl(16, nt),
                    tl(2, 4, h0), tl(2, 4, h1), tl(2, 4, h0), tl(2, 4, h1),
                    tl(2, 4, nt), tl(2, 4, nt), tl(2, 4, nt),
                    tl(2, h0), tl(2, h1), tl(2, h0), tl(2, h1), tl(2, nt), tl(2, nt)]
    scratch += [dma(2, 8, 2), dma(2, 8, 2), dma(2, 3), dma(nch, 2, 20), dma(nch, 2, 20),
                dma(nch, 4), dma(nch, 4), dma(nch, 6), dma(nch, 6), dma(nch, 9), dma(nch, 9),
                dma(nch, 2, 4, 6), dma(nch, 2, 4, 6), dma(nch, 2, 6), dma(nch, 2, 6),
                dma(2, 8, 2), dma(2, 8, 2)]
    w = s((2, HID, DS), BF)
    return pl.pallas_call(
        functools.partial(layer_kernel, cap, chunks, 32 + 20 * sum(len(ch) for _, ch in plans[:index])),
        out_shape=(s((OWN, DM), BF), s((1, OWN), F32), s((OWN, DM), BF), w, w, w),
        in_specs=[pl.BlockSpec(memory_space=pltpu.SMEM), vm, vm, vm, any_, any_, any_],
        out_specs=(vm,) * 6,
        scratch_shapes=scratch,
        compiler_params=pltpu.CompilerParams(
            collective_id=cid, has_side_effects=True, vmem_limit_bytes=VLIM),
        name="layer_%d_%d" % (cap, total),
    )(tab, rows, oc, rw, wg, wu, wd)


def run(rows, oc, rw, counts, tab, wg, wu, wd):
    cap, rmax = 16, ROWS + BR
    rw = rw.reshape(OWN, 1)
    xg, sg = gather_rows(cap, 0, tab, rows, oc, rw)
    part, xc, sc = first_matmuls(cap, rmax, counts, tab, xg, sg, wg, wu, wd)
    h = exchange(rmax, rmax, 1, part)
    o, gr, dg, du, dd = second_matmuls(cap, rmax, counts, tab, h, xc, sc, wg, wu, wd)
    layer_out, grad_weight, grad_rows = reduce_rows(cap, 2, tab, o, gr, rw, oc)
    return layer_out, grad_weight.reshape(1, OWN), grad_rows, dg, du, dd


def per_device(routed_rows, out_cotangent, route_weight, expert_counts, w_gate, w_up, w_down):
    rw = route_weight.reshape(1, OWN)
    wg, wu = jnp.swapaxes(w_gate, 1, 2), jnp.swapaxes(w_up, 1, 2)
    counts = expert_counts.T
    tab = plan_table(PLANS, counts)
    pick = tab[0, 127]

    def fast(i, rows, oc, rw, counts, tab, wg, wu, wd):
        return layer(PLANS, i, 3 + i, tab, rows, oc, rw, wg, wu, wd)

    branches = [functools.partial(fast, i) for i in range(len(PLANS))] + [run]
    layer_out, grad_weight, grad_rows, dg, du, dd = lax.switch(
        pick, branches, routed_rows, out_cotangent, rw, counts, tab, wg, wu, w_down)
    return (layer_out, grad_weight.reshape(OWN), grad_rows,
            jnp.swapaxes(dg, 1, 2), jnp.swapaxes(du, 1, 2), dd)


def solution(mesh):
    return jax.shard_map(
        per_device,
        mesh=mesh,
        in_specs=(
            P(("dp", "et"), None),
            P(("dp", "et"), None),
            P(("dp", "et")),
            P(),
            P(None, None, "et"),
            P(None, None, "et"),
            P(None, "et", None),
        ),
        out_specs=(
            P(("dp", "et"), None),
            P(("dp", "et")),
            P(("dp", "et"), None),
            P(None, "dp", "et"),
            P(None, "dp", "et"),
            P(None, "et", "dp"),
        ),
        check_vma=False,
    )
```
